1024 devices in a mesh: pipe: 16 (over z, x_lo), row: 8 (over x_hi, core), col: 8 (over y).
Axes of the slice: x: 8 (x_hi: 4, x_lo: 2; x = x_hi * 2 + x_lo), y: 8, z: 8, core: 2. Of those that a mesh axis runs over, the one named last changes fastest.
Arguments:
- weights: bfloat16 [16, 4096, 14336], P('pipe', 'col', 'row'), may hold values from -0.09375 to 0.09375
- fwd_resid: bfloat16 [16, 128, 4096], P('pipe', None, 'col'), may hold values from -6 to 6
- fwd_hidden: bfloat16 [16, 128, 14336], P('pipe', None, 'row'), may hold values from -6 to 6
- bwd_resid: bfloat16 [16, 128, 4096], P('pipe', None, 'col'), may hold values from -6 to 6
- bwd_hidden: bfloat16 [16, 128, 14336], P('pipe', None, 'row'), may hold values from -6 to 6
- saved_pre: bfloat16 [4, 16, 128, 14336], P(None, 'pipe', None, 'row'), may hold values from -6 to 6
- pool_embed: bfloat16 [3, 128, 4096], P(None, None, 'col'), may hold values from -6 to 6
- pool_mask: int32 [3, 128], replicated, may hold values 0 or 1
- pool_stratum: int32 [3], replicated, may hold values from 0 to 7
- order: int32 [3], replicated, may hold values from 0 to 2, each once
- mask_vec: bfloat16 [4096], P('col'), may hold values from -6 to 6
- ratio_table: bfloat16 [8, 4096], P(None, 'col'), may hold values from -6 to 6
- cot_inject: bfloat16 [3, 128, 4096], P(None, None, 'col'), may hold values from -6 to 6
Outputs:
- out_resid: bfloat16 [2, 16, 128, 4096], P(None, 'pipe', None, 'col')
- out_hidden: bfloat16 [16, 128, 14336], P('pipe', 'col', 'row')
The draws below stay inside these ranges and needn't reach their ends.
Inputs may be any that keep to these rules, and one draw needn't show every extreme that they name: `order`: each waiting micro-batch enters exactly once.
All inputs are finite; a program needn't handle non-finite values.
Results may differ from the reference program's by a relative error of at most 0.025.
Values may be sent and summed in bfloat16 or wider, within the bound.
A program may use at most 64 MiB of HBM per device.

```python
import jax
import jax.numpy as jnp
from jax import lax

D = 4096
F = 14336
MB_TOK = 128
STEPS = 4
STRATA = 8
POOL = 3
SECTIONS = 16
N_PIPE = 16
N_ROW = 8
N_COL = 8


def touch_ends(drawn, key, least, top_value):
    longest = drawn.shape.index(max(drawn.shape))
    spots = []
    for shift in (0, 1):
        where = [jax.random.randint(jax.random.fold_in(key, axis), (), 0, length) for axis, length in enumerate(drawn.shape)]
        where[longest] = (where[longest] + shift) % drawn.shape[longest]
        spots.append(tuple(where))
    return drawn.at[spots[0]].set(least).at[spots[1]].set(top_value)


def block_scale(rng, extent, pieces, smallest, largest):
    level = 1.0
    for axis_at, parts in pieces:
        steps = jax.random.uniform(jax.random.fold_in(jax.random.fold_in(rng, 6), axis_at), (parts,), jnp.float32, smallest / len(pieces), largest / len(pieces))
        level = level * jnp.repeat(jnp.exp(steps), extent[axis_at] // parts).reshape((-1,) + (1,) * (len(extent) - 1 - axis_at))
    return level


def noise(rng, extent, width, reach, split=(), kind=jnp.bfloat16):
    result = width * jax.random.normal(rng, extent, jnp.float32)
    if split:
        result = result * block_scale(rng, extent, split, -0.22, 0.18)
    return jnp.clip(result, -reach, reach).astype(kind)


def setup_inputs(seed: int = 0) -> dict:
    key_of = jax.random.split(jax.random.key(seed), 14)
    return {
        "weights": noise(key_of[0], (SECTIONS, D, F), D ** -0.5, 0.09375, ((0, 16), (1, 8), (2, 8))),
        "fwd_resid": noise(key_of[1], (SECTIONS, MB_TOK, D), 1.0, 6.0, ((0, 16), (2, 8))),
        "fwd_hidden": noise(key_of[2], (SECTIONS, MB_TOK, F), 1.0, 6.0, ((0, 16), (2, 8))),
        "bwd_resid": noise(key_of[3], (SECTIONS, MB_TOK, D), 1.0, 6.0, ((0, 16), (2, 8))),
        "bwd_hidden": noise(key_of[4], (SECTIONS, MB_TOK, F), 1.0, 6.0, ((0, 16), (2, 8))),
        "saved_pre": noise(key_of[5], (STEPS, SECTIONS, MB_TOK, F), 1.5, 6.0, ((1, 16), (3, 8))),
        "pool_embed": noise(key_of[6], (POOL, MB_TOK, D), 1.0, 6.0, ((2, 8),)),
        "pool_mask": touch_ends((jax.random.randint(key_of[7], (POOL, MB_TOK), 0, 2) < 1).astype(jnp.int32), jax.random.fold_in(key_of[7], 1), 0, 1),
        "pool_stratum": jax.random.randint(key_of[8], (POOL,), 0, STRATA).astype(jnp.int32),
        "order": jax.random.permutation(key_of[9], POOL).astype(jnp.int32),
        "mask_vec": noise(key_of[10], (D,), 1.0, 6.0, ((0, 8),)),
        "ratio_table": noise(key_of[11], (STRATA, D), 1.0, 6.0, ((1, 8),)),
        "cot_inject": noise(key_of[12], (POOL, MB_TOK, D), 1.0, 6.0, ((2, 8),)),
    }


def silu_grad(preact):
    sigma = jax.nn.sigmoid(preact)
    return sigma * (1.0 + preact * (1.0 - sigma))

def sum_features(operand, weight):
    block_width = D // N_COL

    def add_block(block, running):
        offset = (block * block_width).astype(jnp.int32)
        product = jnp.dot(lax.dynamic_slice_in_dim(operand, offset, block_width, 1), lax.dynamic_slice_in_dim(weight, offset, block_width, 0), preferred_element_type=jnp.float32)
        rounded = lax.optimization_barrier(product.astype(jnp.bfloat16))
        return running + rounded.astype(jnp.float32)
    return lax.fori_loop(0, N_COL, add_block, jnp.zeros((operand.shape[0], weight.shape[1]), jnp.float32))

def sum_hidden(operand, weight):
    block_width = F // N_ROW

    def add_block(block, running):
        offset = (block * block_width).astype(jnp.int32)
        product = lax.dot_general(lax.dynamic_slice_in_dim(operand, offset, block_width, 1), lax.dynamic_slice_in_dim(weight, offset, block_width, 1), (((1,), (1,)), ((), ())), preferred_element_type=jnp.float32)
        rounded = lax.optimization_barrier(product.astype(jnp.bfloat16))
        return running + rounded.astype(jnp.float32)
    return lax.fori_loop(0, N_ROW, add_block, jnp.zeros((operand.shape[0], weight.shape[0]), jnp.float32))

def section_update(inputs):
    section, weight, fwd_res, bwd_res, fwd_hid, bwd_hid, saved = inputs
    is_even = section % 2 == 0
    operand = jnp.where(is_even, fwd_res, bwd_res)
    preact = sum_features(operand, weight)
    hid_out = jnp.where(is_even, jax.nn.silu(preact), preact).astype(jnp.bfloat16)
    hid_grad = (bwd_hid.astype(jnp.float32) * silu_grad(saved.astype(jnp.float32))).astype(jnp.bfloat16)
    hid_operand = jnp.where(is_even, hid_grad, fwd_hid)
    residual = jnp.where(is_even, bwd_res, fwd_res)
    updated = (residual.astype(jnp.float32) + sum_hidden(hid_operand, weight)).astype(jnp.bfloat16)
    fwd_out = jnp.where(is_even, fwd_res, updated)
    bwd_out = jnp.where(is_even, updated, bwd_res)
    return (fwd_out, bwd_out, hid_out)

def inject(step_idx, pool_embed, pool_mask, pool_stratum, order, mask_vec, ratio_table):
    chosen = order[step_idx - 1]
    embedded = pool_embed[chosen]
    masked = pool_mask[chosen]
    stratum = pool_stratum[chosen]
    onehot = (jnp.arange(ratio_table.shape[0], dtype=jnp.int32) == stratum).astype(jnp.bfloat16)
    condition = jnp.dot(onehot, ratio_table, preferred_element_type=jnp.float32)
    chosen_rows = jnp.where(masked[:, None] == 1, mask_vec[None, :].astype(jnp.float32), embedded.astype(jnp.float32))
    return (chosen_rows + condition[None, :]).astype(jnp.bfloat16)

def reference(weights, fwd_resid, fwd_hidden, bwd_resid, bwd_hidden, saved_pre, pool_embed, pool_mask, pool_stratum, order, mask_vec, ratio_table, cot_inject):
    section_ids = jnp.arange(N_PIPE, dtype=jnp.int32)
    fwd_res, bwd_res, fwd_hid, bwd_hid = (fwd_resid, bwd_resid, fwd_hidden, bwd_hidden)
    fwd_out, bwd_out, hid_out = (fwd_res, bwd_res, fwd_hid)
    for step_idx in range(STEPS):
        if step_idx > 0:
            incoming = inject(step_idx, pool_embed, pool_mask, pool_stratum, order, mask_vec, ratio_table)
            fwd_res = jnp.concatenate([incoming[None], fwd_out[:-1]], 0)
            fwd_hid = jnp.concatenate([jnp.zeros_like(hid_out[:1]), hid_out[:-1]], 0)
            bwd_res = jnp.concatenate([bwd_out[1:], cot_inject[step_idx - 1][None]], 0)
            bwd_hid = jnp.concatenate([hid_out[1:], jnp.zeros_like(hid_out[:1])], 0)
        fwd_out, bwd_out, hid_out = lax.map(section_update, (section_ids, weights, fwd_res, bwd_res, fwd_hid, bwd_hid, saved_pre[step_idx]))
    return (jnp.stack([fwd_out, bwd_out]), hid_out)
```

```python
import functools

import jax
import jax.numpy as jnp
from jax import lax
from jax.experimental import pallas as pl
from jax.experimental.pallas import tpu as pltpu
from jax.sharding import PartitionSpec as P

MESH = pl.DeviceIdType.MESH
STEPS = 4
F32 = jnp.float32
BF16 = jnp.bfloat16

FAR, IN_UP, IN_DN, NEAR_UP, NEAR_DN, SUM_UP, SUM_DN, SWAP = range(8)
GO_UP1, GO_DN1, GO_UP2, GO_DN2, FWD_UP, FWD_DN, FWD_FAR, RES = range(8, 16)
SPLIT = 16


def relay(
    sizes,
    weights,
    fwd_resid,
    fwd_hidden,
    bwd_resid,
    bwd_hidden,
    saved_pre,
    pool_embed,
    pool_mask,
    pool_stratum,
    order,
    mask_vec,
    ratio_table,
    cot_inject,
    out_resid,
    out_hidden,
    w,
    op,
    res0,
    hin,
    saved0,
    saved,
    embed,
    cot,
    part,
    far,
    inner,
    near,
    summed,
    total,
    hid,
    hid_in,
    blend,
    blend_in,
    res_in,
    upd,
    lsem,
    ssem,
    rsem,
):
    n_pipe, n_row, n_col = sizes
    p, r, c = lax.axis_index("pipe"), lax.axis_index("row"), lax.axis_index("col")
    odd = lax.rem(p, 2)
    even = odd == 0
    c_odd = lax.rem(c, 2)
    tc, tr = hid.shape[1], res_in.shape[1]
    tokens = tc * n_col
    n_hid, n_feat = w.shape[1], w.shape[0]

    def col_at(step):
        return lax.rem(c + (step + n_col), n_col)

    def row_at(step):
        return lax.rem(r + step, n_row)

    def pipe_at(step):
        return lax.rem(p + step + n_pipe, n_pipe)

    partner = p + 1 - 2 * odd
    facing = pipe_at(2 * odd - 1)
    onward = pipe_at(2 - 4 * odd)
    col_far = lax.rem(c + 2 + n_col - 4 * c_odd, n_col)

    barrier = pltpu.get_barrier_semaphore()
    greeted = [{"col": col_at(s)} for s in (1, -1, 2, -2)]
    greeted += [{"pipe": partner}, {"pipe": pipe_at(2)}, {"pipe": pipe_at(-2)}]
    greeted += [{"pipe": facing, "row": row_at(s)} for s in range(n_row)]
    greeted += [{"row": row_at(s)} for s in range(1, n_row)]
    for device in greeted:
        pl.semaphore_signal(barrier, inc=1, device_id=device, device_id_type=MESH)

    def load(slot, src, dst):
        return pltpu.make_async_copy(src, dst, lsem.at[slot])

    row_tile = pl.ds(pl.multiple_of(r * tr, tr), tr)
    col_tile = pl.ds(pl.multiple_of(c * tc, tc), tc)
    get_w = load(0, weights.at[0], w)
    get_op = load(1, fwd_resid.at[0], op.at[0])
    get_op_odd = load(1, bwd_resid.at[0], op.at[0])
    get_res = load(2, bwd_resid.at[0, row_tile], res0)
    get_res_odd = load(2, fwd_resid.at[0, row_tile], res0)
    get_hin = load(3, bwd_hidden.at[0], hin.at[0])
    get_hin_odd = load(3, fwd_hidden.at[0], hin.at[0])
    get_saved0 = load(4, saved_pre.at[0, 0], saved0)
    get_saved = load(5, saved_pre.at[pl.ds(1, STEPS - 1), 0, col_tile], saved)
    get_embed = load(6, pool_embed.at[:, row_tile], embed)
    get_cot = load(7, cot_inject.at[:, row_tile], cot)

    get_w.start()

    @pl.when(even)
    def _():
        get_op.start()
        get_hin.start()
        get_res.start()

    @pl.when(odd == 1)
    def _():
        get_op_odd.start()
        get_hin_odd.start()
        get_res_odd.start()

    get_saved0.start()
    get_saved.start()
    get_embed.start()
    get_cot.start()

    started = []

    def send(k, number, src, dst, device):
        copy = pltpu.make_async_remote_copy(
            src_ref=src,
            dst_ref=dst,
            send_sem=ssem.at[k, number],
            recv_sem=rsem.at[k, number],
            device_id=device,
            device_id_type=MESH,
        )
        copy.start()
        started.append(copy)
        return copy

    def col_view(x):
        return x.reshape(n_col, tc, x.shape[-1])

    def multiply_up(k):
        for at in range(0, n_hid, 256):
            cols = pl.ds(at, min(256, n_hid - at))
            out = jnp.dot(op[k], w[:, cols], preferred_element_type=F32)
            part[k, :, :, cols] = col_view(out.astype(BF16))

    def multiply_down(k):
        for at in range(0, n_feat, 256):
            cols = pl.ds(at, min(256, n_feat - at))
            out = lax.dot_general(
                hin[k], w[cols, :], (((1,), (1,)), ((), ())), preferred_element_type=F32
            )
            blend[k, :, :, cols] = out.astype(BF16).reshape(n_row, tr, -1)

    def hin_tile(k, t):
        return hin.at[k, pl.ds(pl.multiple_of(t * tc, tc), tc)]

    def sum_start(k):
        a = send(k, FAR, part.at[k, col_at(4)], far.at[k], {"col": col_far})
        b = send(k, IN_UP, part.at[k, col_at(3)], inner.at[k, 0], {"col": col_at(1)})
        d = send(k, IN_DN, part.at[k, col_at(-3)], inner.at[k, 1], {"col": col_at(-1)})
        e = send(k, NEAR_UP, part.at[k, col_at(1)], near.at[k, 0], {"col": col_at(1)})
        f = send(k, NEAR_DN, part.at[k, col_at(-1)], near.at[k, 1], {"col": col_at(-1)})
        return a, b, d, e, f

    def sum_middle(k, arriving):
        for copy in arriving[:3]:
            copy.wait_recv()
        from_far = far[k].astype(F32)
        up = part[k, col_at(2)].astype(F32) + inner[k, 0].astype(F32)
        summed[k, 0] = (up + jnp.where(c_odd == 0, from_far, 0.0)).astype(BF16)
        a = send(k, SUM_UP, summed.at[k, 0], total.at[k, 0], {"col": col_at(2)})
        down = part[k, col_at(-2)].astype(F32) + inner[k, 1].astype(F32)
        summed[k, 1] = (down + jnp.where(c_odd == 0, 0.0, from_far)).astype(BF16)
        b = send(k, SUM_DN, summed.at[k, 1], total.at[k, 1], {"col": col_at(-2)})
        return arriving[3], arriving[4], a, b

    def sum_end(k, arriving):
        for copy in arriving:
            copy.wait_recv()
        pre = part[k, c].astype(F32) + near[k, 0].astype(F32) + near[k, 1].astype(F32)
        pre = pre + total[k, 0].astype(F32) + total[k, 1].astype(F32)
        return jnp.where(even, pre / (1.0 + jnp.exp(-pre)), pre).astype(BF16)

    def swap_start(k, value):
        hid[k] = value
        return send(k, SWAP, hid.at[k], hid_in.at[k], {"pipe": partner})

    def slope(a):
        s = 1.0 / (1.0 + jnp.exp(-a))
        return s * (1.0 + a * (1.0 - s))

    def swap_end(k, arriving):
        arriving.wait_recv()
        gate = jnp.where(even, slope(saved[k].astype(F32)), 1.0)
        mine = hin_tile(k + 1, c)
        mine[...] = (hid_in[k].astype(F32) * gate).astype(BF16)
        return (
            send(k, GO_UP2, mine, mine, {"col": col_at(2)}),
            send(k, GO_DN2, mine, mine, {"col": col_at(-2)}),
            send(k, GO_UP1, mine, mine, {"col": col_at(1)}),
            send(k, GO_DN1, mine, mine, {"col": col_at(-1)}),
        )

    def forward(k, arriving):
        arriving[0].wait_recv()
        arriving[1].wait_recv()
        below, above = hin_tile(k + 1, col_at(-2)), hin_tile(k + 1, col_at(2))
        far_tile = hin_tile(k + 1, lax.rem(c + n_col - 2 + 4 * c_odd, n_col))
        return (
            send(k, FWD_FAR, far_tile, far_tile, {"col": col_far}),
            send(k, FWD_UP, below, below, {"col": col_at(1)}),
            send(k, FWD_DN, above, above, {"col": col_at(-1)}),
            arriving[2],
            arriving[3],
        )

    def blend_start(k):
        last = k == STEPS - 1
        copies = []
        if last:
            tile = op.at[k - 1, row_tile]
            copies.append(send(k, RES, tile, res_in.at[k], {"pipe": partner}))
        for s in range(1 if last else 0, n_row):
            row = row_at(s)
            device = {"row": row} if last else {"pipe": facing, "row": row}
            copies.append(send(k, SPLIT + s, blend.at[k, row], blend_in.at[k, s], device))
        return copies

    def blend_end(k, arriving):
        last = k == STEPS - 1
        for copy in arriving:
            copy.wait_recv()
        new = res_in[k].astype(F32)
        if last:
            new = new + blend[k, r].astype(F32)
        for s in range(1 if last else 0, n_row):
            new = new + blend_in[k, s].astype(F32)
        if not last:
            new = jnp.where(p == 0, injected(k), new)
            new = jnp.where(p == n_pipe - 1, cot[k].astype(F32), new)
        dst = upd if last else op.at[k + 1]
        mine = dst.at[row_tile]
        mine[...] = new.astype(BF16)
        return [
            send(k, SPLIT + n_row + s, mine, mine, {"row": row_at(s)}) for s in range(1, n_row)
        ]

    def pick(index, ref):
        value = ref[ref.shape[0] - 1]
        for i in range(ref.shape[0] - 1):
            value = jnp.where(index == i, ref[i], value)
        return value

    def injected(k):
        chosen = order[k]
        stratum = pick(chosen, pool_stratum)
        mask = pool_mask[pl.ds(pool_mask.shape[0] - 1, 1), :]
        for i in range(pool_mask.shape[0] - 1):
            mask = jnp.where(chosen == i, pool_mask[pl.ds(i, 1), :], mask)
        here = lax.broadcasted_iota(jnp.int32, (tr, tokens), 0) + r * tr
        there = lax.broadcasted_iota(jnp.int32, (tr, tokens), 1)
        column = jnp.where(here == there, jnp.broadcast_to(mask, (tr, tokens)), 0)
        masked = jnp.sum(column.astype(F32), axis=1, keepdims=True) == 1.0
        table = ratio_table[...].astype(F32)
        strata = lax.broadcasted_iota(jnp.int32, table.shape, 0)
        condition = jnp.sum(jnp.where(strata == stratum, table, 0.0), axis=0, keepdims=True)
        vec = jnp.broadcast_to(mask_vec[...].astype(F32), (tr, n_feat))
        rows = jnp.where(masked, vec, pick(chosen, embed).astype(F32))
        return rows + condition

    def wait_all(copies):
        for copy in copies:
            copy.wait_recv()

    get_op.wait()
    get_w.wait()
    multiply_up(0)
    pl.semaphore_wait(barrier, len(greeted))
    x = sum_start(0)

    get_hin.wait()
    get_saved0.wait()
    gate = jnp.where(even, slope(saved0[...].astype(F32)), 1.0)
    hin[0] = (hin[0].astype(F32) * gate).astype(BF16)
    multiply_down(0)
    get_res.wait()
    y = blend_start(0)
    y.append(send(0, RES, res0, res_in.at[0], {"pipe": facing}))
    get_saved.wait()
    get_embed.wait()
    get_cot.wait()

    def send_res(k):
        tile = op.at[k, row_tile]
        return send(k + 1, RES, tile, res_in.at[k + 1], {"pipe": onward})

    res = send_res(0)
    x = sum_middle(0, x)
    y = blend_end(0, y)
    x = swap_start(0, sum_end(0, x))
    x = swap_end(0, x)
    wait_all(y)
    multiply_up(1)
    y = sum_start(1)
    next_res = send_res(1)
    x = forward(0, x)
    y = sum_middle(1, y)
    wait_all(x)
    multiply_down(1)
    x = blend_start(1) + [res]
    y = swap_start(1, sum_end(1, y))
    y = swap_end(1, y)
    x = blend_end(1, x)
    y = forward(1, y)
    wait_all(x)
    multiply_up(2)
    x = sum_start(2)
    wait_all(y)
    multiply_down(2)
    y = blend_start(2) + [next_res]
    x = sum_middle(2, x)
    y = blend_end(2, y)
    x = swap_start(2, sum_end(2, x))
    x = swap_end(2, x)
    wait_all(y)
    multiply_up(3)
    y = sum_start(3)
    out_resid[odd, 0] = op[3]
    x = forward(2, x)
    y = sum_middle(3, y)
    wait_all(x)
    multiply_down(3)
    x = blend_start(3)
    out_hidden[0] = sum_end(3, y)
    x = blend_end(3, x)
    wait_all(x)
    out_resid[1 - odd, 0] = upd[...]
    for copy in started:
        copy.wait_send()


def solution(mesh):
    sizes = tuple(mesh.shape[a] for a in ("pipe", "row", "col"))
    n_pipe, n_row, n_col = sizes

    def shards(weights, fwd_resid, fwd_hidden, *rest):
        _, tokens, n_feat = fwd_resid.shape
        n_hid = fwd_hidden.shape[2]
        tc, tr = tokens // n_col, tokens // n_row
        pool = rest[3].shape[0]
        args = [weights, fwd_resid, fwd_hidden, *rest]
        args[10] = args[10].reshape(1, n_feat)
        hbm = pl.BlockSpec(memory_space=pl.ANY)
        vmem = pl.BlockSpec(memory_space=pltpu.VMEM)
        smem = pl.BlockSpec(memory_space=pltpu.SMEM)
        in_specs = [hbm] * 7 + [vmem, smem, smem, vmem, vmem, hbm]
        copies = SPLIT + 2 * n_row
        return pl.pallas_call(
            functools.partial(relay, sizes),
            out_shape=(
                jax.ShapeDtypeStruct((2, 1, tokens, n_feat), BF16),
                jax.ShapeDtypeStruct((1, tc, n_hid), BF16),
            ),
            in_specs=in_specs,
            out_specs=(vmem, vmem),
            scratch_shapes=[
                pltpu.VMEM((n_feat, n_hid), BF16),
                pltpu.VMEM((STEPS, tokens, n_feat), BF16),
                pltpu.VMEM((tr, n_feat), BF16),
                pltpu.VMEM((STEPS, tokens, n_hid), BF16),
                pltpu.VMEM((tokens, n_hid), BF16),
                pltpu.VMEM((STEPS - 1, tc, n_hid), BF16),
                pltpu.VMEM((pool, tr, n_feat), BF16),
                pltpu.VMEM((pool, tr, n_feat), BF16),
                pltpu.VMEM((STEPS, n_col, tc, n_hid), BF16),
                pltpu.VMEM((STEPS, tc, n_hid), BF16),
                pltpu.VMEM((STEPS, 2, tc, n_hid), BF16),
                pltpu.VMEM((STEPS, 2, tc, n_hid), BF16),
                pltpu.VMEM((STEPS, 2, tc, n_hid), BF16),
                pltpu.VMEM((STEPS, 2, tc, n_hid), BF16),
                pltpu.VMEM((STEPS, tc, n_hid), BF16),
                pltpu.VMEM((STEPS, tc, n_hid), BF16),
                pltpu.VMEM((STEPS, n_row, tr, n_feat), BF16),
                pltpu.VMEM((STEPS, n_row, tr, n_feat), BF16),
                pltpu.VMEM((STEPS, tr, n_feat), BF16),
                pltpu.VMEM((tokens, n_feat), BF16),
                pltpu.SemaphoreType.DMA((8,)),
                pltpu.SemaphoreType.DMA((STEPS, copies)),
                pltpu.SemaphoreType.DMA((STEPS, copies)),
            ],
            compiler_params=pltpu.CompilerParams(
                collective_id=0, has_side_effects=True, vmem_limit_bytes=48 * 2**20
            ),
        )(*args)

    return jax.shard_map(
        shards,
        mesh=mesh,
        in_specs=(
            P("pipe", "col", "row"),
            P("pipe", None, "col"),
            P("pipe", None, "row"),
            P("pipe", None, "col"),
            P("pipe", None, "row"),
            P(None, "pipe", None, "row"),
            P(None, None, "col"),
            P(),
            P(),
            P(),
            P("col"),
            P(None, "col"),
            P(None, None, "col"),
        ),
        out_specs=(P(None, "pipe", None, "col"), P("pipe", "col", "row")),
        check_vma=False,
    )
```

```python
import functools

import jax
import jax.numpy as jnp
from jax import lax
from jax.experimental import pallas as pl
from jax.experimental.pallas import tpu as pltpu
from jax.sharding import PartitionSpec as P

MESH = pl.DeviceIdType.MESH
STEPS = 4
F32 = jnp.float32
BF16 = jnp.bfloat16

FAR, IN_UP, IN_DN, NEAR_UP, NEAR_DN, SUM_UP, SUM_DN, SWAP = range(8)
GO_UP1, GO_DN1, GO_UP2, GO_DN2, FWD_UP, FWD_DN, FWD_FAR, RES = range(8, 16)
SPLIT = 16


def relay(
    sizes,
    weights,
    fwd_resid,
    fwd_hidden,
    bwd_resid,
    bwd_hidden,
    saved_pre,
    pool_embed,
    pool_mask,
    pool_stratum,
    order,
    mask_vec,
    ratio_table,
    cot_inject,
    out_resid,
    out_hidden,
    w,
    op,
    res0,
    hin,
    saved0,
    saved,
    embed,
    cot,
    mask_in,
    stratum_in,
    order_in,
    vec_in,
    table_in,
    part,
    far,
    inner,
    near,
    summed,
    total,
    hid,
    hid_in,
    blend,
    blend_in,
    res_in,
    upd,
    lsem,
    ssem,
    rsem,
):
    n_pipe, n_row, n_col = sizes
    p, r, c = lax.axis_index("pipe"), lax.axis_index("row"), lax.axis_index("col")
    odd = lax.rem(p, 2)
    even = odd == 0
    c_odd = lax.rem(c, 2)
    tc, tr = hid.shape[1], res_in.shape[1]
    tokens = tc * n_col
    n_hid, n_feat = w.shape[1], w.shape[0]

    def col_at(step):
        return lax.rem(c + (step + n_col), n_col)

    def row_at(step):
        return lax.rem(r + step, n_row)

    def pipe_at(step):
        return lax.rem(p + step + n_pipe, n_pipe)

    partner = p + 1 - 2 * odd
    facing = pipe_at(2 * odd - 1)
    onward = pipe_at(2 - 4 * odd)
    col_far = lax.rem(c + 2 + n_col - 4 * c_odd, n_col)

    barrier = pltpu.get_barrier_semaphore()
    greeted = [{"col": col_at(s)} for s in (1, -1, 2, -2)]
    greeted += [{"pipe": partner}, {"pipe": pipe_at(2)}, {"pipe": pipe_at(-2)}]
    greeted += [{"pipe": facing, "row": row_at(s)} for s in range(n_row)]
    greeted += [{"row": row_at(s)} for s in range(1, n_row)]
    for device in greeted:
        pl.semaphore_signal(barrier, inc=1, device_id=device, device_id_type=MESH)

    def load(slot, src, dst):
        return pltpu.make_async_copy(src, dst, lsem.at[slot])

    row_tile = pl.ds(pl.multiple_of(r * tr, tr), tr)
    col_tile = pl.ds(pl.multiple_of(c * tc, tc), tc)
    get_w = load(0, weights.at[0], w)
    get_op = load(1, fwd_resid.at[0], op.at[0])
    get_op_odd = load(1, bwd_resid.at[0], op.at[0])
    get_res = load(2, bwd_resid.at[0, row_tile], res0)
    get_res_odd = load(2, fwd_resid.at[0, row_tile], res0)
    get_hin = load(3, bwd_hidden.at[0], hin.at[0])
    get_hin_odd = load(3, fwd_hidden.at[0], hin.at[0])
    get_saved0 = load(4, saved_pre.at[0, 0], saved0)
    get_saved = load(5, saved_pre.at[pl.ds(1, STEPS - 1), 0, col_tile], saved)

    get_w.start()

    @pl.when(even)
    def _():
        get_op.start()
        get_hin.start()
        get_saved0.start()
        get_res.start()

    @pl.when(odd == 1)
    def _():
        get_op_odd.start()
        get_hin_odd.start()
        get_res_odd.start()

    get_saved.start()
    small = [
        load(6, pool_embed.at[:, row_tile], embed),
        load(7, cot_inject.at[:, row_tile], cot),
        load(8, pool_mask, mask_in),
        load(9, pool_stratum, stratum_in),
        load(10, order, order_in),
        load(11, mask_vec, vec_in),
        load(12, ratio_table, table_in),
    ]
    for copy in small:
        copy.start()

    started = []

    def send(k, number, src, dst, device):
        copy = pltpu.make_async_remote_copy(
            src_ref=src,
            dst_ref=dst,
            send_sem=ssem.at[k, number],
            recv_sem=rsem.at[k, number],
            device_id=device,
            device_id_type=MESH,
        )
        copy.start()
        started.append(copy)
        return copy

    def col_view(x):
        return x.reshape(n_col, tc, x.shape[-1])

    def multiply_up(k):
        for at in range(0, n_hid, 256):
            cols = pl.ds(at, min(256, n_hid - at))
            out = jnp.dot(op[k], w[:, cols], preferred_element_type=F32)
            part[k, :, :, cols] = col_view(out.astype(BF16))

    def multiply_down(k):
        for at in range(0, n_feat, 256):
            cols = pl.ds(at, min(256, n_feat - at))
            out = lax.dot_general(
                hin[k], w[cols, :], (((1,), (1,)), ((), ())), preferred_element_type=F32
            )
            blend[k, :, :, cols] = out.astype(BF16).reshape(n_row, tr, -1)

    def hin_tile(k, t):
        return hin.at[k, pl.ds(pl.multiple_of(t * tc, tc), tc)]

    def sum_start(k):
        a = send(k, FAR, part.at[k, col_at(4)], far.at[k], {"col": col_far})
        b = send(k, IN_UP, part.at[k, col_at(3)], inner.at[k, 0], {"col": col_at(1)})
        d = send(k, IN_DN, part.at[k, col_at(-3)], inner.at[k, 1], {"col": col_at(-1)})
        e = send(k, NEAR_UP, part.at[k, col_at(1)], near.at[k, 0], {"col": col_at(1)})
        f = send(k, NEAR_DN, part.at[k, col_at(-1)], near.at[k, 1], {"col": col_at(-1)})
        return a, b, d, e, f

    def sum_middle(k, arriving):
        for copy in arriving[:3]:
            copy.wait_recv()
        from_far = far[k].astype(F32)
        up = part[k, col_at(2)].astype(F32) + inner[k, 0].astype(F32)
        summed[k, 0] = (up + jnp.where(c_odd == 0, from_far, 0.0)).astype(BF16)
        a = send(k, SUM_UP, summed.at[k, 0], total.at[k, 0], {"col": col_at(2)})
        down = part[k, col_at(-2)].astype(F32) + inner[k, 1].astype(F32)
        summed[k, 1] = (down + jnp.where(c_odd == 0, 0.0, from_far)).astype(BF16)
        b = send(k, SUM_DN, summed.at[k, 1], total.at[k, 1], {"col": col_at(-2)})
        return arriving[3], arriving[4], a, b

    def sum_end(k, arriving):
        for copy in arriving:
            copy.wait_recv()
        pre = part[k, c].astype(F32) + near[k, 0].astype(F32) + near[k, 1].astype(F32)
        pre = pre + total[k, 0].astype(F32) + total[k, 1].astype(F32)
        return jnp.where(even, pre / (1.0 + jnp.exp(-pre)), pre).astype(BF16)

    def swap_start(k, value):
        hid[k] = value
        return send(k, SWAP, hid.at[k], hid_in.at[k], {"pipe": partner})

    def slope(a):
        s = 1.0 / (1.0 + jnp.exp(-a))
        return s * (1.0 + a * (1.0 - s))

    def swap_end(k, arriving):
        arriving.wait_recv()
        gate = jnp.where(even, slope(saved[k].astype(F32)), 1.0)
        mine = hin_tile(k + 1, c)
        mine[...] = (hid_in[k].astype(F32) * gate).astype(BF16)
        return (
            send(k, GO_UP2, mine, mine, {"col": col_at(2)}),
            send(k, GO_DN2, mine, mine, {"col": col_at(-2)}),
            send(k, GO_UP1, mine, mine, {"col": col_at(1)}),
            send(k, GO_DN1, mine, mine, {"col": col_at(-1)}),
        )

    def forward(k, arriving):
        arriving[0].wait_recv()
        arriving[1].wait_recv()
        below, above = hin_tile(k + 1, col_at(-2)), hin_tile(k + 1, col_at(2))
        far_tile = hin_tile(k + 1, lax.rem(c + n_col - 2 + 4 * c_odd, n_col))
        return (
            send(k, FWD_FAR, far_tile, far_tile, {"col": col_far}),
            send(k, FWD_UP, below, below, {"col": col_at(1)}),
            send(k, FWD_DN, above, above, {"col": col_at(-1)}),
            arriving[2],
            arriving[3],
        )

    def blend_start(k):
        last = k == STEPS - 1
        copies = []
        if last:
            tile = op.at[k - 1, row_tile]
            copies.append(send(k, RES, tile, res_in.at[k], {"pipe": partner}))
        for s in range(1 if last else 0, n_row):
            row = row_at(s)
            device = {"row": row} if last else {"pipe": facing, "row": row}
            copies.append(send(k, SPLIT + s, blend.at[k, row], blend_in.at[k, s], device))
        return copies

    def blend_end(k, arriving):
        last = k == STEPS - 1
        for copy in arriving:
            copy.wait_recv()
        new = res_in[k].astype(F32)
        if last:
            new = new + blend[k, r].astype(F32)
        for s in range(1 if last else 0, n_row):
            new = new + blend_in[k, s].astype(F32)
        if not last:
            new = jnp.where(p == 0, injected(k), new)
            new = jnp.where(p == n_pipe - 1, cot[k].astype(F32), new)
        dst = upd if last else op.at[k + 1]
        mine = dst.at[row_tile]
        mine[...] = new.astype(BF16)
        return [
            send(k, SPLIT + n_row + s, mine, mine, {"row": row_at(s)}) for s in range(1, n_row)
        ]

    def pick(index, ref):
        value = ref[ref.shape[0] - 1]
        for i in range(ref.shape[0] - 1):
            value = jnp.where(index == i, ref[i], value)
        return value

    def injected(k):
        chosen = order_in[k]
        stratum = pick(chosen, stratum_in)
        mask = mask_in[pl.ds(mask_in.shape[0] - 1, 1), :]
        for i in range(mask_in.shape[0] - 1):
            mask = jnp.where(chosen == i, mask_in[pl.ds(i, 1), :], mask)
        here = lax.broadcasted_iota(jnp.int32, (tr, tokens), 0) + r * tr
        there = lax.broadcasted_iota(jnp.int32, (tr, tokens), 1)
        column = jnp.where(here == there, jnp.broadcast_to(mask, (tr, tokens)), 0)
        masked = jnp.sum(column.astype(F32), axis=1, keepdims=True) == 1.0
        table = table_in[...].astype(F32)
        strata = lax.broadcasted_iota(jnp.int32, table.shape, 0)
        condition = jnp.sum(jnp.where(strata == stratum, table, 0.0), axis=0, keepdims=True)
        vec = jnp.broadcast_to(vec_in[...].astype(F32)[None], (tr, n_feat))
        rows = jnp.where(masked, vec, pick(chosen, embed).astype(F32))
        return rows + condition

    def wait_all(copies):
        for copy in copies:
            copy.wait_recv()

    get_op.wait()
    get_w.wait()
    multiply_up(0)
    pl.semaphore_wait(barrier, len(greeted))
    x = sum_start(0)

    get_hin.wait()

    @pl.when(even)
    def _():
        get_saved0.wait()
        hin[0] = (hin[0].astype(F32) * slope(saved0[...].astype(F32))).astype(BF16)

    multiply_down(0)
    get_res.wait()
    y = blend_start(0)
    y.append(send(0, RES, res0, res_in.at[0], {"pipe": facing}))
    get_saved.wait()
    for copy in small:
        copy.wait()

    def send_res(k):
        tile = op.at[k, row_tile]
        return send(k + 1, RES, tile, res_in.at[k + 1], {"pipe": onward})

    res = send_res(0)
    x = sum_middle(0, x)
    y = blend_end(0, y)
    x = swap_start(0, sum_end(0, x))
    x = swap_end(0, x)
    wait_all(y)
    multiply_up(1)
    y = sum_start(1)
    next_res = send_res(1)
    x = forward(0, x)
    y = sum_middle(1, y)
    wait_all(x)
    multiply_down(1)
    x = blend_start(1) + [res]
    y = swap_start(1, sum_end(1, y))
    y = swap_end(1, y)
    x = blend_end(1, x)
    y = forward(1, y)
    wait_all(x)
    multiply_up(2)
    x = sum_start(2)
    wait_all(y)
    multiply_down(2)
    y = blend_start(2) + [next_res]
    x = sum_middle(2, x)
    y = blend_end(2, y)
    x = swap_start(2, sum_end(2, x))
    x = swap_end(2, x)
    wait_all(y)
    multiply_up(3)
    y = sum_start(3)
    out_resid[odd, 0] = op[3]
    x = forward(2, x)
    y = sum_middle(3, y)
    wait_all(x)
    multiply_down(3)
    x = blend_start(3)
    out_hidden[0] = sum_end(3, y)
    x = blend_end(3, x)
    wait_all(x)
    out_resid[1 - odd, 0] = upd[...]
    for copy in started:
        copy.wait_send()


def solution(mesh):
    sizes = tuple(mesh.shape[a] for a in ("pipe", "row", "col"))
    n_pipe, n_row, n_col = sizes

    def shards(weights, fwd_resid, fwd_hidden, *rest):
        _, tokens, n_feat = fwd_resid.shape
        n_hid = fwd_hidden.shape[2]
        tc, tr = tokens // n_col, tokens // n_row
        pool = rest[3].shape[0]
        hbm = pl.BlockSpec(memory_space=pl.ANY)
        vmem = pl.BlockSpec(memory_space=pltpu.VMEM)
        copies = SPLIT + 2 * n_row
        return pl.pallas_call(
            functools.partial(relay, sizes),
            out_shape=(
                jax.ShapeDtypeStruct((2, 1, tokens, n_feat), BF16),
                jax.ShapeDtypeStruct((1, tc, n_hid), BF16),
            ),
            in_specs=[hbm] * 13,
            out_specs=(vmem, vmem),
            scratch_shapes=[
                pltpu.VMEM((n_feat, n_hid), BF16),
                pltpu.VMEM((STEPS, tokens, n_feat), BF16),
                pltpu.VMEM((tr, n_feat), BF16),
                pltpu.VMEM((STEPS, tokens, n_hid), BF16),
                pltpu.VMEM((tokens, n_hid), BF16),
                pltpu.VMEM((STEPS - 1, tc, n_hid), BF16),
                pltpu.VMEM((pool, tr, n_feat), BF16),
                pltpu.VMEM((pool, tr, n_feat), BF16),
                pltpu.VMEM((pool, tokens), jnp.int32),
                pltpu.SMEM((pool,), jnp.int32),
                pltpu.SMEM((pool,), jnp.int32),
                pltpu.VMEM((n_feat,), BF16),
                pltpu.VMEM((rest[8].shape[0], n_feat), BF16),
                pltpu.VMEM((STEPS, n_col, tc, n_hid), BF16),
                pltpu.VMEM((STEPS, tc, n_hid), BF16),
                pltpu.VMEM((STEPS, 2, tc, n_hid), BF16),
                pltpu.VMEM((STEPS, 2, tc, n_hid), BF16),
                pltpu.VMEM((STEPS, 2, tc, n_hid), BF16),
                pltpu.VMEM((STEPS, 2, tc, n_hid), BF16),
                pltpu.VMEM((STEPS, tc, n_hid), BF16),
                pltpu.VMEM((STEPS, tc, n_hid), BF16),
                pltpu.VMEM((STEPS, n_row, tr, n_feat), BF16),
                pltpu.VMEM((STEPS, n_row, tr, n_feat), BF16),
                pltpu.VMEM((STEPS, tr, n_feat), BF16),
                pltpu.VMEM((tokens, n_feat), BF16),
                pltpu.SemaphoreType.DMA((13,)),
                pltpu.SemaphoreType.DMA((STEPS, copies)),
                pltpu.SemaphoreType.DMA((STEPS, copies)),
            ],
            compiler_params=pltpu.CompilerParams(
                collective_id=0, has_side_effects=True, vmem_limit_bytes=60 * 1024 * 1024
            ),
        )(weights, fwd_resid, fwd_hidden, *rest)

    return jax.shard_map(
        shards,
        mesh=mesh,
        in_specs=(
            P("pipe", "col", "row"),
            P("pipe", None, "col"),
            P("pipe", None, "row"),
            P("pipe", None, "col"),
            P("pipe", None, "row"),
            P(None, "pipe", None, "row"),
            P(None, None, "col"),
            P(),
            P(),
            P(),
            P("col"),
            P(None, "col"),
            P(None, None, "col"),
        ),
        out_specs=(P(None, "pipe", None, "col"), P("pipe", "col", "row")),
        check_vma=False,
    )
```

```python
import functools

import jax
import jax.numpy as jnp
from jax import lax
from jax.experimental import pallas as pl
from jax.experimental.pallas import tpu as pltpu
from jax.sharding import PartitionSpec as P

MESH = pl.DeviceIdType.MESH
STEPS = 4
F32 = jnp.float32
BF16 = jnp.bfloat16

FAR, IN_UP, IN_DN, NEAR_UP, NEAR_DN, SUM_UP, SUM_DN, SUM_OWN = range(8)
GO_UP1, GO_DN1, GO_UP2, GO_DN2, FWD_UP, FWD_DN, FWD_FAR = range(8, 15)
PER_RUN = 15


def runs_of(n_hid):
    half = (n_hid // 2 + 255) // 256 * 256 if n_hid > 256 else 128
    return ((0, half), (half, n_hid - half))


def relay(
    sizes,
    weights,
    fwd_resid,
    fwd_hidden,
    bwd_resid,
    bwd_hidden,
    saved_pre,
    pool_embed,
    pool_mask,
    pool_stratum,
    order,
    mask_vec,
    ratio_table,
    cot_inject,
    out_resid,
    out_hidden,
    w,
    op,
    res0,
    hin,
    saved0,
    saved,
    embed,
    cot,
    mask_in,
    stratum_in,
    order_in,
    vec_in,
    table_in,
    part,
    far,
    inner,
    near,
    summed,
    total,
    down,
    blend,
    mate_in,
    pair,
    blend_in,
    res_in,
    upd,
    lsem,
    ssem,
    rsem,
):
    n_pipe, n_row, n_col = sizes
    p, r, c = lax.axis_index("pipe"), lax.axis_index("row"), lax.axis_index("col")
    odd = lax.rem(p, 2)
    even = odd == 0
    c_odd = lax.rem(c, 2)
    tc, tr = far.shape[1], res_in.shape[1]
    tokens = tc * n_col
    n_hid, n_feat = w.shape[1], w.shape[0]
    runs = runs_of(n_hid)
    whole = range(len(runs))
    lanes = [pl.ds(at, width) for at, width in runs]
    RES = PER_RUN * len(runs)
    MATE, SPLIT = RES + 1, RES + 3
    SPREAD = SPLIT + n_row // 2
    core, chip, n_chip = lax.rem(r, 2), r // 2, n_row // 2

    def col_at(step):
        return lax.rem(c + (step + n_col), n_col)

    def chip_at(step):
        return lax.rem(chip + step, n_chip)

    def pipe_at(step):
        return lax.rem(p + step + n_pipe, n_pipe)

    partner = p + 1 - 2 * odd
    facing = pipe_at(2 * odd - 1)
    onward = pipe_at(2 - 4 * odd)
    col_far = lax.rem(c + 2 + n_col - 4 * c_odd, n_col)

    barrier = pltpu.get_barrier_semaphore()
    greeted = [{"col": col_at(s)} for s in (1, -1, 2, -2)]
    greeted += [{"pipe": partner, "col": col_at(s)} for s in (0, 2, -2)]
    greeted += [{"pipe": pipe_at(s)} for s in (2, -2)]
    greeted += [{"pipe": facing, "row": 2 * chip_at(s) + core} for s in range(n_chip)]
    greeted += [{"row": lax.rem(r + s, n_row)} for s in range(1, n_row)]
    for device in greeted:
        pl.semaphore_signal(barrier, inc=1, device_id=device, device_id_type=MESH)

    def load(slot, src, dst):
        return pltpu.make_async_copy(src, dst, lsem.at[slot])

    row_tile = pl.ds(pl.multiple_of(r * tr, tr), tr)
    col_tile = pl.ds(pl.multiple_of(c * tc, tc), tc)
    get_w = load(0, weights.at[0], w)
    get_op = load(1, fwd_resid.at[0], op.at[0])
    get_op_odd = load(1, bwd_resid.at[0], op.at[0])
    get_res = load(2, bwd_resid.at[0, row_tile], res0)
    get_res_odd = load(2, fwd_resid.at[0, row_tile], res0)
    get_hin = load(3, bwd_hidden.at[0], hin.at[0])
    get_hin_odd = load(3, fwd_hidden.at[0], hin.at[0])
    get_saved0 = load(4, saved_pre.at[0, 0], saved0)
    get_saved = load(5, saved_pre.at[pl.ds(1, STEPS - 1), 0, col_tile], saved)

    get_w.start()

    @pl.when(even)
    def _():
        get_op.start()
        get_hin.start()
        get_saved0.start()
        get_res.start()

    @pl.when(odd == 1)
    def _():
        get_op_odd.start()
        get_hin_odd.start()
        get_res_odd.start()

    get_saved.start()
    small = [
        load(6, pool_embed.at[:, row_tile], embed),
        load(7, cot_inject.at[:, row_tile], cot),
        load(8, pool_mask, mask_in),
        load(9, pool_stratum, stratum_in),
        load(10, order, order_in),
        load(11, mask_vec, vec_in),
        load(12, ratio_table, table_in),
    ]
    for copy in small:
        copy.start()

    started = []

    def send(k, number, src, dst, device):
        copy = pltpu.make_async_remote_copy(
            src_ref=src,
            dst_ref=dst,
            send_sem=ssem.at[k, number],
            recv_sem=rsem.at[k, number],
            device_id=device,
            device_id_type=MESH,
        )
        copy.start()
        started.append(copy)
        return copy

    def col_view(x):
        return x.reshape(n_col, tc, x.shape[-1])

    def multiply_up(k, h):
        start, width = runs[h]
        for at in range(start, start + width, 256):
            cols = pl.ds(at, min(256, start + width - at))
            out = jnp.dot(op[k], w[:, cols], preferred_element_type=F32)
            part[k, :, :, cols] = col_view(out.astype(BF16))

    def multiply_down(k, h, cols):
        out = lax.dot_general(
            hin[k, :, lanes[h]],
            w[cols, lanes[h]],
            (((1,), (1,)), ((), ())),
            preferred_element_type=F32,
        )
        if h > 0:
            out = out + down[:, cols]
        if h < len(runs) - 1:
            down[:, cols] = out
        else:
            out = out.reshape(n_chip, 2, tr, out.shape[1])
            blend[k, :, :, :, cols] = out.astype(BF16)

    def hin_tile(k, t, h):
        return hin.at[k, pl.ds(pl.multiple_of(t * tc, tc), tc), lanes[h]]

    def share(k, h, number, step, dst, to):
        src = part.at[k, col_at(step), :, lanes[h]]
        return send(k, PER_RUN * h + number, src, dst, {"col": to})

    def sum_start(k, h):
        return (
            share(k, h, FAR, 4, far.at[k, :, lanes[h]], col_far),
            share(k, h, IN_UP, 3, inner.at[k, 0, :, lanes[h]], col_at(1)),
            share(k, h, IN_DN, -3, inner.at[k, 1, :, lanes[h]], col_at(-1)),
        )

    def sum_near(k, h):
        return (
            share(k, h, NEAR_UP, 1, near.at[k, 0, :, lanes[h]], col_at(1)),
            share(k, h, NEAR_DN, -1, near.at[k, 1, :, lanes[h]], col_at(-1)),
        )

    def sum_send(k, h, number, slot, value, step):
        summed[k, slot, :, lanes[h]] = value.astype(BF16)
        src, dst = summed.at[k, slot, :, lanes[h]], total.at[k, slot, :, lanes[h]]
        device = {"col": col_at(step)}
        if k < STEPS - 1:
            device["pipe"] = partner
        return send(k, PER_RUN * h + number, src, dst, device)

    def sum_middle(k, h, arriving):
        ready(arriving)
        run = lanes[h]
        from_far = far[k, :, run].astype(F32)
        up = part[k, col_at(2), :, run].astype(F32) + inner[k, 0, :, run].astype(F32)
        up = up + jnp.where(c_odd == 0, from_far, 0.0)
        a = sum_send(k, h, SUM_UP, 0, up, 2)
        low = part[k, col_at(-2), :, run].astype(F32) + inner[k, 1, :, run].astype(F32)
        low = low + jnp.where(c_odd == 0, 0.0, from_far)
        b = sum_send(k, h, SUM_DN, 1, low, -2)
        return a, b

    def sum_own(k, h, arriving):
        ready(arriving)
        run = lanes[h]
        own = part[k, c, :, run].astype(F32) + near[k, 0, :, run].astype(F32)
        own = own + near[k, 1, :, run].astype(F32)
        if k < STEPS - 1:
            return (sum_send(k, h, SUM_OWN, 2, own, 0),)
        summed[k, 2, :, run] = own.astype(BF16)
        return ()

    def silu(v):
        return v / (1.0 + jnp.exp(-v))

    def sum_end(k, h, arriving):
        ready(arriving)
        run = lanes[h]
        own = summed if k == STEPS - 1 else total
        pre = own[k, 2, :, run].astype(F32)
        pre = pre + total[k, 0, :, run].astype(F32) + total[k, 1, :, run].astype(F32)
        from_even = even if k == STEPS - 1 else odd == 1
        return jnp.where(from_even, silu(pre), pre).astype(BF16)

    def slope(a):
        s = 1.0 / (1.0 + jnp.exp(-a))
        return s * (1.0 + a * (1.0 - s))

    def pass_on(k, h, number, tile, to):
        return send(k, PER_RUN * h + number, tile, tile, {"col": to})

    def go_far(k, h, arriving):
        value = sum_end(k, h, arriving).astype(F32)
        gate = jnp.where(even, slope(saved[k, :, lanes[h]].astype(F32)), 1.0)
        mine = hin_tile(k + 1, c, h)
        mine[...] = (value * gate).astype(BF16)
        return (
            pass_on(k, h, GO_UP2, mine, col_at(2)),
            pass_on(k, h, GO_DN2, mine, col_at(-2)),
        )

    def go_near(k, h):
        mine = hin_tile(k + 1, c, h)
        return (
            pass_on(k, h, GO_UP1, mine, col_at(1)),
            pass_on(k, h, GO_DN1, mine, col_at(-1)),
        )

    def forward(k, h, arriving):
        ready(arriving)
        below = hin_tile(k + 1, col_at(-2), h)
        above = hin_tile(k + 1, col_at(2), h)
        far_tile = hin_tile(k + 1, lax.rem(c + n_col - 2 + 4 * c_odd, n_col), h)
        return (
            pass_on(k, h, FWD_FAR, far_tile, col_far),
            pass_on(k, h, FWD_UP, below, col_at(1)),
            pass_on(k, h, FWD_DN, above, col_at(-1)),
        )

    def chip_steps(last):
        if n_chip != 4:
            return list(range(1 if last else 0, n_chip))
        return [2, 1, 3] if last else [2, 1 + 2 * odd, 0, 3 - 2 * odd]

    def mate_start(k):
        copies = []
        for n in range(2):
            cols = pl.ds(n * (n_feat // 2), n_feat // 2)
            multiply_down(k, len(runs) - 1, cols)
            src, dst = blend.at[k, :, 1 - core, :, cols], mate_in.at[k, :, :, cols]
            copies.append(send(k, MATE + n, src, dst, {"row": r + 1 - 2 * core}))
        return copies

    def blend_start(k, arriving):
        last = k == STEPS - 1
        ready(arriving)
        both = blend[k, :, core].astype(F32) + mate_in[k].astype(F32)
        pair[k] = both.astype(BF16)
        copies = []
        for i, s in enumerate(chip_steps(last)):
            to = chip_at(s)
            device = {"row": 2 * to + core}
            if not last:
                device["pipe"] = facing
            copies.append(send(k, SPLIT + i, pair.at[k, to], blend_in.at[k, i], device))
        return copies

    def blend_end(k, arriving):
        last = k == STEPS - 1
        ready(arriving)
        new = res_in[k].astype(F32)
        if last:
            new = new + pair[k, chip].astype(F32)
        for i in range(len(chip_steps(last))):
            new = new + blend_in[k, i].astype(F32)
        if not last:
            new = jnp.where(p == 0, injected(k), new)
            new = jnp.where(p == n_pipe - 1, cot[k].astype(F32), new)
        dst = upd if last else op.at[k + 1]
        mine = dst.at[row_tile]
        mine[...] = new.astype(BF16)
        copies = []
        for s in [2, 1, 3, 0] if n_chip == 4 else range(n_chip):
            for other in (0, 1) if s else (1,):
                to = 2 * chip_at(s) + core + other * (1 - 2 * core)
                copies.append(send(k, SPREAD + 2 * s + other, mine, mine, {"row": to}))
        return copies

    def pick(index, ref):
        value = ref[ref.shape[0] - 1]
        for i in range(ref.shape[0] - 1):
            value = jnp.where(index == i, ref[i], value)
        return value

    def injected(k):
        chosen = order_in[k]
        stratum = pick(chosen, stratum_in)
        mask = mask_in[pl.ds(mask_in.shape[0] - 1, 1), :]
        for i in range(mask_in.shape[0] - 1):
            mask = jnp.where(chosen == i, mask_in[pl.ds(i, 1), :], mask)
        here = lax.broadcasted_iota(jnp.int32, (tr, tokens), 0) + r * tr
        there = lax.broadcasted_iota(jnp.int32, (tr, tokens), 1)
        column = jnp.where(here == there, jnp.broadcast_to(mask, (tr, tokens)), 0)
        masked = jnp.sum(column.astype(F32), axis=1, keepdims=True) == 1.0
        table = table_in[...].astype(F32)
        strata = lax.broadcasted_iota(jnp.int32, table.shape, 0)
        condition = jnp.sum(jnp.where(strata == stratum, table, 0.0), axis=0, keepdims=True)
        vec = jnp.broadcast_to(vec_in[...].astype(F32)[None], (tr, n_feat))
        rows = jnp.where(masked, vec, pick(chosen, embed).astype(F32))
        return rows + condition

    def ready(copies):
        for copy in copies:
            copy.wait_recv()

    def starts(k):
        return [sum_start(k, h) for h in whole]

    def nears(k):
        return [sum_near(k, h) for h in whole]

    def ups(k):
        for h in whole:
            multiply_up(k, h)

    def middles(k, arriving, beside):
        sums = [sum_middle(k, h, arriving[h]) for h in whole]
        return [sums[h] + sum_own(k, h, beside[h]) for h in whole]

    def gathers(k, arriving):
        return [go_far(k, h, arriving[h]) for h in whole]

    def goes(k):
        return [go_near(k, h) for h in whole]

    def forwards(k, arriving):
        return [forward(k, h, arriving[h]) for h in whole]

    def mates(k, arriving, beside):
        for h in whole:
            ready(arriving[h] + beside[h])
            if h < len(runs) - 1:
                for n in range(2):
                    multiply_down(k, h, pl.ds(n * (n_feat // 2), n_feat // 2))
        return mate_start(k)

    def send_res(k):
        to = partner if k == STEPS - 2 else onward
        return [send(k + 1, RES, op.at[k, row_tile], res_in.at[k + 1], {"pipe": to})]

    nothing = [(), ()]
    get_op.wait()
    get_w.wait()
    ups(0)
    pl.semaphore_wait(barrier, len(greeted))
    x = starts(0)
    xn = nears(0)
    get_hin.wait()

    @pl.when(even)
    def _():
        get_saved0.wait()
        hin[0] = (hin[0].astype(F32) * slope(saved0[...].astype(F32))).astype(BF16)

    y = mates(0, nothing, nothing)
    get_res.wait()
    y_res = [send(0, RES, res0, res_in.at[0], {"pipe": facing})]
    y = blend_start(0, y)
    x_res = send_res(0)
    get_saved.wait()
    for copy in small:
        copy.wait()
    x = middles(0, x, xn)
    x = gathers(0, x)
    xn = goes(0)
    y = blend_end(0, y + y_res)
    x = forwards(0, x)
    ready(y)
    ups(1)
    y = starts(1)
    yn = nears(1)
    y_res = send_res(1)
    x = mates(1, x, xn)
    x = blend_start(1, x)
    y = middles(1, y, yn)
    x = blend_end(1, x + x_res)
    y = gathers(1, y)
    yn = goes(1)
    ready(x)
    ups(2)
    x = starts(2)
    y = forwards(1, y)
    xn = nears(2)
    x_res = send_res(2)
    x = middles(2, x, xn)
    y = mates(2, y, yn)
    y = blend_start(2, y)
    x = gathers(2, x)
    xn = goes(2)
    y = blend_end(2, y + y_res)
    x = forwards(2, x)
    ready(y)
    ups(3)
    y = starts(3)
    yn = nears(3)
    out_resid[odd, 0] = op[3]
    x = mates(3, x, xn)
    x = blend_start(3, x)
    y = middles(3, y, yn)
    for h in whole:
        out_hidden[0, :, lanes[h]] = sum_end(3, h, y[h])
    x = blend_end(3, x + x_res)
    ready(x)
    out_resid[1 - odd, 0] = upd[...]
    for copy in started:
        copy.wait_send()


def solution(mesh):
    sizes = tuple(mesh.shape[a] for a in ("pipe", "row", "col"))
    n_pipe, n_row, n_col = sizes

    def shards(weights, fwd_resid, fwd_hidden, *rest):
        _, tokens, n_feat = fwd_resid.shape
        n_hid = fwd_hidden.shape[2]
        tc, tr = tokens // n_col, tokens // n_row
        pool = rest[3].shape[0]
        hbm = pl.BlockSpec(memory_space=pltpu.HBM)
        vmem = pl.BlockSpec(memory_space=pltpu.VMEM)
        n_chip = n_row // 2
        copies = PER_RUN * len(runs_of(n_hid)) + 3 + n_chip + n_row
        return pl.pallas_call(
            functools.partial(relay, sizes),
            out_shape=(
                jax.ShapeDtypeStruct((2, 1, tokens, n_feat), BF16),
                jax.ShapeDtypeStruct((1, tc, n_hid), BF16),
            ),
            in_specs=[hbm] * 13,
            out_specs=(vmem, vmem),
            scratch_shapes=[
                pltpu.VMEM((n_feat, n_hid), BF16),
                pltpu.VMEM((STEPS, tokens, n_feat), BF16),
                pltpu.VMEM((tr, n_feat), BF16),
                pltpu.VMEM((STEPS, tokens, n_hid), BF16),
                pltpu.VMEM((tokens, n_hid), BF16),
                pltpu.VMEM((STEPS - 1, tc, n_hid), BF16),
                pltpu.VMEM((pool, tr, n_feat), BF16),
                pltpu.VMEM((pool, tr, n_feat), BF16),
                pltpu.VMEM((pool, tokens), jnp.int32),
                pltpu.SMEM((pool,), jnp.int32),
                pltpu.SMEM((pool,), jnp.int32),
                pltpu.VMEM((n_feat,), BF16),
                pltpu.VMEM((rest[8].shape[0], n_feat), BF16),
                pltpu.VMEM((STEPS, n_col, tc, n_hid), BF16),
                pltpu.VMEM((STEPS, tc, n_hid), BF16),
                pltpu.VMEM((STEPS, 2, tc, n_hid), BF16),
                pltpu.VMEM((STEPS, 2, tc, n_hid), BF16),
                pltpu.VMEM((STEPS, 3, tc, n_hid), BF16),
                pltpu.VMEM((STEPS, 3, tc, n_hid), BF16),
                pltpu.VMEM((tokens, n_feat), F32),
                pltpu.VMEM((STEPS, n_chip, 2, tr, n_feat), BF16),
                pltpu.VMEM((STEPS, n_chip, tr, n_feat), BF16),
                pltpu.VMEM((STEPS, n_chip, tr, n_feat), BF16),
                pltpu.VMEM((STEPS, n_chip, tr, n_feat), BF16),
                pltpu.VMEM((STEPS, tr, n_feat), BF16),
                pltpu.VMEM((tokens, n_feat), BF16),
                pltpu.SemaphoreType.DMA((13,)),
                pltpu.SemaphoreType.DMA((STEPS, copies)),
                pltpu.SemaphoreType.DMA((STEPS, copies)),
            ],
            compiler_params=pltpu.CompilerParams(
                collective_id=0, has_side_effects=True, vmem_limit_bytes=60 * 1024 * 1024
            ),
        )(weights, fwd_resid, fwd_hidden, *rest)

    return jax.shard_map(
        shards,
        mesh=mesh,
        in_specs=(
            P("pipe", "col", "row"),
            P("pipe", None, "col"),
            P("pipe", None, "row"),
            P("pipe", None, "col"),
            P("pipe", None, "row"),
            P(None, "pipe", None, "row"),
            P(None, None, "col"),
            P(),
            P(),
            P(),
            P("col"),
            P(None, "col"),
            P(None, None, "col"),
        ),
        out_specs=(P(None, "pipe", None, "col"), P("pipe", "col", "row")),
        check_vma=False,
    )
```

```python
import functools

import jax
import jax.numpy as jnp
from jax import lax
from jax.experimental import pallas as pl
from jax.experimental.pallas import tpu as pltpu
from jax.sharding import PartitionSpec as P

MESH = pl.DeviceIdType.MESH
STEPS = 4
F32 = jnp.float32
BF16 = jnp.bfloat16

FAR, IN_UP, IN_DN, NEAR_UP, NEAR_DN, SUM_UP, SUM_DN, SUM_OWN = range(8)
GO_UP1, GO_DN1, GO_UP2, GO_DN2, FWD_UP, FWD_DN, FWD_FAR = range(8, 15)
PER_RUN = 15


def runs_of(n_hid):
    half = (n_hid // 2 + 255) // 256 * 256 if n_hid > 256 else 128
    return ((0, half), (half, n_hid - half))


def relay(
    sizes,
    weights,
    fwd_resid,
    fwd_hidden,
    bwd_resid,
    bwd_hidden,
    saved_pre,
    pool_embed,
    pool_mask,
    pool_stratum,
    order,
    mask_vec,
    ratio_table,
    cot_inject,
    out_resid,
    out_hidden,
    w,
    op,
    res0,
    hin,
    saved0,
    saved,
    embed,
    cot,
    mask_in,
    stratum_in,
    order_in,
    vec_in,
    table_in,
    part,
    far,
    inner,
    near,
    summed,
    total,
    down,
    blend,
    mate_in,
    pair,
    blend_in,
    res_in,
    upd,
    lsem,
    ssem,
    rsem,
):
    n_pipe, n_row, n_col = sizes
    p, r, c = lax.axis_index("pipe"), lax.axis_index("row"), lax.axis_index("col")
    odd = lax.rem(p, 2)
    even = odd == 0
    c_odd = lax.rem(c, 2)
    tc, tr = far.shape[1], res_in.shape[1]
    tokens = tc * n_col
    n_hid, n_feat = w.shape[1], w.shape[0]
    runs = runs_of(n_hid)
    whole = range(len(runs))
    lanes = [pl.ds(at, width) for at, width in runs]
    RES = PER_RUN * len(runs)
    MATE, SPLIT = RES + 1, RES + 3
    SPREAD = SPLIT + n_row // 2
    core, chip, n_chip = lax.rem(r, 2), r // 2, n_row // 2

    def col_at(step):
        return lax.rem(c + (step + n_col), n_col)

    def chip_at(step):
        return lax.rem(chip + step, n_chip)

    def pipe_at(step):
        return lax.rem(p + step + n_pipe, n_pipe)

    partner = p + 1 - 2 * odd
    facing = pipe_at(2 * odd - 1)
    onward = pipe_at(2 - 4 * odd)
    col_far = lax.rem(c + 2 + n_col - 4 * c_odd, n_col)

    inside = (p > 0) & (p < n_pipe - 1)
    above, below = p < n_pipe - 2, p > 1
    has_onward = (p != 1) & (p != n_pipe - 2)

    barrier = pltpu.get_barrier_semaphore()
    greeted = [{"col": col_at(s)} for s in (1, -1, 2, -2)]
    greeted += [{"pipe": partner, "col": col_at(s)} for s in (0, 2, -2)]
    greeted += [{"row": lax.rem(r + s, n_row)} for s in range(1, n_row)]
    across = [{"pipe": facing, "row": 2 * chip_at(s) + core} for s in range(n_chip)]

    def greet(devices):
        for device in devices:
            pl.semaphore_signal(barrier, inc=1, device_id=device, device_id_type=MESH)

    pl.when(inside)(lambda: greet(across))
    pl.when(above)(lambda: greet([{"pipe": pipe_at(2)}]))
    pl.when(below)(lambda: greet([{"pipe": pipe_at(-2)}]))
    greet(greeted)
    greetings = len(greeted) + jnp.where(inside, n_chip, 0)
    greetings = greetings + jnp.where(above, 1, 0) + jnp.where(below, 1, 0)

    def load(slot, src, dst):
        return pltpu.make_async_copy(src, dst, lsem.at[slot])

    row_tile = pl.ds(pl.multiple_of(r * tr, tr), tr)
    col_tile = pl.ds(pl.multiple_of(c * tc, tc), tc)
    get_w = load(0, weights.at[0], w)
    get_op = load(1, fwd_resid.at[0], op.at[0])
    get_op_odd = load(1, bwd_resid.at[0], op.at[0])
    get_res = load(2, bwd_resid.at[0, row_tile], res0)
    get_res_odd = load(2, fwd_resid.at[0, row_tile], res0)
    get_hin = load(3, bwd_hidden.at[0], hin.at[0])
    get_hin_odd = load(3, fwd_hidden.at[0], hin.at[0])
    get_saved0 = load(4, saved_pre.at[0, 0], saved0)
    get_saved = load(5, saved_pre.at[pl.ds(1, STEPS - 1), 0, col_tile], saved)

    get_w.start()

    @pl.when(even)
    def _():
        get_op.start()
        get_hin.start()
        get_saved0.start()
        get_res.start()

    @pl.when(odd == 1)
    def _():
        get_op_odd.start()
        get_hin_odd.start()
        get_res_odd.start()

    get_saved.start()
    small = [
        load(6, pool_embed.at[:, row_tile], embed),
        load(7, cot_inject.at[:, row_tile], cot),
        load(8, pool_mask, mask_in),
        load(9, pool_stratum, stratum_in),
        load(10, order, order_in),
        load(11, mask_vec, vec_in),
        load(12, ratio_table, table_in),
    ]
    for copy in small:
        copy.start()

    started = []

    def send(k, number, src, dst, device, when=None):
        copy = pltpu.make_async_remote_copy(
            src_ref=src,
            dst_ref=dst,
            send_sem=ssem.at[k, number],
            recv_sem=rsem.at[k, number],
            device_id=device,
            device_id_type=MESH,
        )
        if when is None:
            copy.start()
        else:
            pl.when(when)(copy.start)
        started.append((copy, when))
        return copy

    def col_view(x):
        return x.reshape(n_col, tc, x.shape[-1])

    def multiply_up(k, h):
        start, width = runs[h]
        for at in range(start, start + width, 256):
            cols = pl.ds(at, min(256, start + width - at))
            out = jnp.dot(op[k], w[:, cols], preferred_element_type=F32)
            part[k, :, :, cols] = col_view(out.astype(BF16))

    def multiply_down(k, h, cols):
        out = lax.dot_general(
            hin[k, :, lanes[h]],
            w[cols, lanes[h]],
            (((1,), (1,)), ((), ())),
            preferred_element_type=F32,
        )
        if h > 0:
            out = out + down[:, cols]
        if h < len(runs) - 1:
            down[:, cols] = out
        else:
            out = out.reshape(n_chip, 2, tr, out.shape[1])
            blend[k, :, :, :, cols] = out.astype(BF16)

    def hin_tile(k, t, h):
        return hin.at[k, pl.ds(pl.multiple_of(t * tc, tc), tc), lanes[h]]

    def share(k, h, number, step, dst, to):
        src = part.at[k, col_at(step), :, lanes[h]]
        return send(k, PER_RUN * h + number, src, dst, {"col": to})

    def sum_start(k, h):
        return (
            share(k, h, FAR, 4, far.at[k, :, lanes[h]], col_far),
            share(k, h, IN_UP, 3, inner.at[k, 0, :, lanes[h]], col_at(1)),
            share(k, h, IN_DN, -3, inner.at[k, 1, :, lanes[h]], col_at(-1)),
        )

    def sum_near(k, h):
        return (
            share(k, h, NEAR_UP, 1, near.at[k, 0, :, lanes[h]], col_at(1)),
            share(k, h, NEAR_DN, -1, near.at[k, 1, :, lanes[h]], col_at(-1)),
        )

    def sum_send(k, h, number, slot, value, step):
        summed[k, slot, :, lanes[h]] = value.astype(BF16)
        src, dst = summed.at[k, slot, :, lanes[h]], total.at[k, slot, :, lanes[h]]
        device = {"col": col_at(step)}
        if k < STEPS - 1:
            device["pipe"] = partner
        return send(k, PER_RUN * h + number, src, dst, device)

    def sum_middle(k, h, arriving):
        ready(arriving)
        run = lanes[h]
        from_far = far[k, :, run].astype(F32)
        up = part[k, col_at(2), :, run].astype(F32) + inner[k, 0, :, run].astype(F32)
        up = up + jnp.where(c_odd == 0, from_far, 0.0)
        a = sum_send(k, h, SUM_UP, 0, up, 2)
        low = part[k, col_at(-2), :, run].astype(F32) + inner[k, 1, :, run].astype(F32)
        low = low + jnp.where(c_odd == 0, 0.0, from_far)
        b = sum_send(k, h, SUM_DN, 1, low, -2)
        return a, b

    def sum_own(k, h, arriving):
        ready(arriving)
        run = lanes[h]
        own = part[k, c, :, run].astype(F32) + near[k, 0, :, run].astype(F32)
        own = own + near[k, 1, :, run].astype(F32)
        if k < STEPS - 1:
            return (sum_send(k, h, SUM_OWN, 2, own, 0),)
        summed[k, 2, :, run] = own.astype(BF16)
        return ()

    def silu(v):
        return v / (1.0 + jnp.exp(-v))

    def sum_end(k, h, arriving):
        ready(arriving)
        run = lanes[h]
        own = summed if k == STEPS - 1 else total
        pre = own[k, 2, :, run].astype(F32)
        pre = pre + total[k, 0, :, run].astype(F32) + total[k, 1, :, run].astype(F32)
        from_even = even if k == STEPS - 1 else odd == 1
        return jnp.where(from_even, silu(pre), pre).astype(BF16)

    def slope(a):
        s = 1.0 / (1.0 + jnp.exp(-a))
        return s * (1.0 + a * (1.0 - s))

    def pass_on(k, h, number, tile, to):
        return send(k, PER_RUN * h + number, tile, tile, {"col": to})

    def go_far(k, h, arriving):
        value = sum_end(k, h, arriving).astype(F32)
        gate = jnp.where(even, slope(saved[k, :, lanes[h]].astype(F32)), 1.0)
        mine = hin_tile(k + 1, c, h)
        mine[...] = (value * gate).astype(BF16)
        return (
            pass_on(k, h, GO_UP2, mine, col_at(2)),
            pass_on(k, h, GO_DN2, mine, col_at(-2)),
        )

    def go_near(k, h):
        mine = hin_tile(k + 1, c, h)
        return (
            pass_on(k, h, GO_UP1, mine, col_at(1)),
            pass_on(k, h, GO_DN1, mine, col_at(-1)),
        )

    def forward(k, h, arriving):
        ready(arriving)
        below = hin_tile(k + 1, col_at(-2), h)
        above = hin_tile(k + 1, col_at(2), h)
        far_tile = hin_tile(k + 1, lax.rem(c + n_col - 2 + 4 * c_odd, n_col), h)
        return (
            pass_on(k, h, FWD_FAR, far_tile, col_far),
            pass_on(k, h, FWD_UP, below, col_at(1)),
            pass_on(k, h, FWD_DN, above, col_at(-1)),
        )

    def chip_steps(last):
        if n_chip != 4:
            return list(range(1 if last else 0, n_chip))
        return [2, 1, 3] if last else [2, 1 + 2 * odd, 0, 3 - 2 * odd]

    def mate_start(k):
        copies = []
        for n in range(2):
            cols = pl.ds(n * (n_feat // 2), n_feat // 2)
            multiply_down(k, len(runs) - 1, cols)
            src, dst = blend.at[k, :, 1 - core, :, cols], mate_in.at[k, :, :, cols]
            copies.append(send(k, MATE + n, src, dst, {"row": r + 1 - 2 * core}))
        return copies

    def blend_start(k, arriving):
        last = k == STEPS - 1
        ready(arriving)
        both = blend[k, :, core].astype(F32) + mate_in[k].astype(F32)
        pair[k] = both.astype(BF16)
        copies = []
        for i, s in enumerate(chip_steps(last)):
            to = chip_at(s)
            device = {"row": 2 * to + core}
            if not last:
                device["pipe"] = facing
            src, dst = pair.at[k, to], blend_in.at[k, i]
            copies.append(send(k, SPLIT + i, src, dst, device, None if last else inside))
        return copies

    def blend_end(k, arriving):
        last = k == STEPS - 1
        mine = (upd if last else op.at[k + 1]).at[row_tile]

        def finish():
            ready(arriving)
            new = res_in[k].astype(F32)
            if last:
                new = new + pair[k, chip].astype(F32)
            for i in range(len(chip_steps(last))):
                new = new + blend_in[k, i].astype(F32)
            mine[...] = new.astype(BF16)

        if last:
            finish()
        else:
            pl.when(inside)(finish)

            @pl.when(p == 0)
            def _():
                mine[...] = injected(k).astype(BF16)

            @pl.when(p == n_pipe - 1)
            def _():
                mine[...] = cot[k]

        copies = []
        for s in [2, 1, 3, 0] if n_chip == 4 else range(n_chip):
            for other in (0, 1) if s else (1,):
                to = 2 * chip_at(s) + core + other * (1 - 2 * core)
                copies.append(send(k, SPREAD + 2 * s + other, mine, mine, {"row": to}))
        return copies

    def pick(index, ref):
        value = ref[ref.shape[0] - 1]
        for i in range(ref.shape[0] - 1):
            value = jnp.where(index == i, ref[i], value)
        return value

    def injected(k):
        chosen = order_in[k]
        stratum = pick(chosen, stratum_in)
        mask = mask_in[pl.ds(mask_in.shape[0] - 1, 1), :]
        for i in range(mask_in.shape[0] - 1):
            mask = jnp.where(chosen == i, mask_in[pl.ds(i, 1), :], mask)
        here = lax.broadcasted_iota(jnp.int32, (tr, tokens), 0) + r * tr
        there = lax.broadcasted_iota(jnp.int32, (tr, tokens), 1)
        column = jnp.where(here == there, jnp.broadcast_to(mask, (tr, tokens)), 0)
        masked = jnp.sum(column.astype(F32), axis=1, keepdims=True) == 1.0
        table = table_in[...].astype(F32)
        strata = lax.broadcasted_iota(jnp.int32, table.shape, 0)
        condition = jnp.sum(jnp.where(strata == stratum, table, 0.0), axis=0, keepdims=True)
        vec = jnp.broadcast_to(vec_in[...].astype(F32)[None], (tr, n_feat))
        rows = jnp.where(masked, vec, pick(chosen, embed).astype(F32))
        return rows + condition

    def ready(copies):
        for copy in copies:
            copy.wait_recv()

    def starts(k):
        return [sum_start(k, h) for h in whole]

    def nears(k):
        return [sum_near(k, h) for h in whole]

    def ups(k):
        for h in whole:
            multiply_up(k, h)

    def middles(k, arriving, beside):
        sums = [sum_middle(k, h, arriving[h]) for h in whole]
        return [sums[h] + sum_own(k, h, beside[h]) for h in whole]

    def gathers(k, arriving):
        return [go_far(k, h, arriving[h]) for h in whole]

    def goes(k):
        return [go_near(k, h) for h in whole]

    def forwards(k, arriving):
        return [forward(k, h, arriving[h]) for h in whole]

    def mates(k, arriving, beside):
        for h in whole:
            ready(arriving[h] + beside[h])
            if h < len(runs) - 1:
                for n in range(2):
                    multiply_down(k, h, pl.ds(n * (n_feat // 2), n_feat // 2))
        return mate_start(k)

    def send_res(k):
        src, dst = op.at[k, row_tile], res_in.at[k + 1]
        if k == STEPS - 2:
            return [send(k + 1, RES, src, dst, {"pipe": partner})]
        return [send(k + 1, RES, src, dst, {"pipe": onward}, has_onward)]

    nothing = [(), ()]
    get_op.wait()
    get_w.wait()
    ups(0)
    pl.semaphore_wait(barrier, greetings)
    x = starts(0)
    xn = nears(0)
    get_hin.wait()

    @pl.when(even)
    def _():
        get_saved0.wait()
        hin[0] = (hin[0].astype(F32) * slope(saved0[...].astype(F32))).astype(BF16)

    y = mates(0, nothing, nothing)
    get_res.wait()
    y_res = [send(0, RES, res0, res_in.at[0], {"pipe": facing}, inside)]
    y = blend_start(0, y)
    x_res = send_res(0)
    get_saved.wait()
    for copy in small:
        copy.wait()
    x = middles(0, x, xn)
    x = gathers(0, x)
    xn = goes(0)
    y = blend_end(0, y + y_res)
    x = forwards(0, x)
    ready(y)
    ups(1)
    y = starts(1)
    yn = nears(1)
    y_res = send_res(1)
    x = mates(1, x, xn)
    x = blend_start(1, x)
    y = middles(1, y, yn)
    x = blend_end(1, x + x_res)
    y = gathers(1, y)
    yn = goes(1)
    ready(x)
    ups(2)
    x = starts(2)
    xn = nears(2)
    y = forwards(1, y)
    x_res = send_res(2)
    x = middles(2, x, xn)
    y = mates(2, y, yn)
    y = blend_start(2, y)
    x = gathers(2, x)
    xn = goes(2)
    y = blend_end(2, y + y_res)
    x = forwards(2, x)
    ready(y)
    ups(3)
    y = starts(3)
    yn = nears(3)
    out_resid[odd, 0] = op[3]
    x = mates(3, x, xn)
    x = blend_start(3, x)
    y = middles(3, y, yn)
    for h in whole:
        out_hidden[0, :, lanes[h]] = sum_end(3, h, y[h])
    x = blend_end(3, x + x_res)
    ready(x)
    out_resid[1 - odd, 0] = upd[...]
    for copy, when in started:
        if when is None:
            copy.wait_send()
        else:
            pl.when(when)(copy.wait_send)


def solution(mesh):
    sizes = tuple(mesh.shape[a] for a in ("pipe", "row", "col"))
    n_pipe, n_row, n_col = sizes

    def shards(weights, fwd_resid, fwd_hidden, *rest):
        _, tokens, n_feat = fwd_resid.shape
        n_hid = fwd_hidden.shape[2]
        tc, tr = tokens // n_col, tokens // n_row
        pool = rest[3].shape[0]
        hbm = pl.BlockSpec(memory_space=pltpu.HBM)
        vmem = pl.BlockSpec(memory_space=pltpu.VMEM)
        n_chip = n_row // 2
        copies = PER_RUN * len(runs_of(n_hid)) + 3 + n_chip + n_row
        return pl.pallas_call(
            functools.partial(relay, sizes),
            out_shape=(
                jax.ShapeDtypeStruct((2, 1, tokens, n_feat), BF16),
                jax.ShapeDtypeStruct((1, tc, n_hid), BF16),
            ),
            in_specs=[hbm] * 13,
            out_specs=(vmem, vmem),
            scratch_shapes=[
                pltpu.VMEM((n_feat, n_hid), BF16),
                pltpu.VMEM((STEPS, tokens, n_feat), BF16),
                pltpu.VMEM((tr, n_feat), BF16),
                pltpu.VMEM((STEPS, tokens, n_hid), BF16),
                pltpu.VMEM((tokens, n_hid), BF16),
                pltpu.VMEM((STEPS - 1, tc, n_hid), BF16),
                pltpu.VMEM((pool, tr, n_feat), BF16),
                pltpu.VMEM((pool, tr, n_feat), BF16),
                pltpu.VMEM((pool, tokens), jnp.int32),
                pltpu.SMEM((pool,), jnp.int32),
                pltpu.SMEM((pool,), jnp.int32),
                pltpu.VMEM((n_feat,), BF16),
                pltpu.VMEM((rest[8].shape[0], n_feat), BF16),
                pltpu.VMEM((STEPS, n_col, tc, n_hid), BF16),
                pltpu.VMEM((STEPS, tc, n_hid), BF16),
                pltpu.VMEM((STEPS, 2, tc, n_hid), BF16),
                pltpu.VMEM((STEPS, 2, tc, n_hid), BF16),
                pltpu.VMEM((STEPS, 3, tc, n_hid), BF16),
                pltpu.VMEM((STEPS, 3, tc, n_hid), BF16),
                pltpu.VMEM((tokens, n_feat), F32),
                pltpu.VMEM((STEPS, n_chip, 2, tr, n_feat), BF16),
                pltpu.VMEM((STEPS, n_chip, tr, n_feat), BF16),
                pltpu.VMEM((STEPS, n_chip, tr, n_feat), BF16),
                pltpu.VMEM((STEPS, n_chip, tr, n_feat), BF16),
                pltpu.VMEM((STEPS, tr, n_feat), BF16),
                pltpu.VMEM((tokens, n_feat), BF16),
                pltpu.SemaphoreType.DMA((13,)),
                pltpu.SemaphoreType.DMA((STEPS, copies)),
                pltpu.SemaphoreType.DMA((STEPS, copies)),
            ],
            compiler_params=pltpu.CompilerParams(
                collective_id=0, has_side_effects=True, vmem_limit_bytes=60 * 1024 * 1024
            ),
        )(weights, fwd_resid, fwd_hidden, *rest)

    return jax.shard_map(
        shards,
        mesh=mesh,
        in_specs=(
            P("pipe", "col", "row"),
            P("pipe", None, "col"),
            P("pipe", None, "row"),
            P("pipe", None, "col"),
            P("pipe", None, "row"),
            P(None, "pipe", None, "row"),
            P(None, None, "col"),
            P(),
            P(),
            P(),
            P("col"),
            P(None, "col"),
            P(None, None, "col"),
        ),
        out_specs=(P(None, "pipe", None, "col"), P("pipe", "col", "row")),
        check_vma=False,
    )
```

```python
import functools

import jax
import jax.numpy as jnp
from jax import lax
from jax.experimental import pallas as pl
from jax.experimental.pallas import tpu as pltpu
from jax.sharding import PartitionSpec as P

MESH = pl.DeviceIdType.MESH
STEPS = 4
F32 = jnp.float32
BF16 = jnp.bfloat16

FAR, IN_UP, IN_DN, NEAR_UP, NEAR_DN, SUM_UP, SUM_DN, SUM_OWN = range(8)
GO_UP1, GO_DN1, GO_UP2, GO_DN2, FWD_UP, FWD_DN, FWD_FAR = range(8, 15)
PER_RUN = 15


def runs_of(n_hid):
    half = (n_hid // 2 + 255) // 256 * 256 if n_hid > 256 else 128
    return ((0, half), (half, n_hid - half))


def relay(
    sizes,
    weights,
    fwd_resid,
    fwd_hidden,
    bwd_resid,
    bwd_hidden,
    saved_pre,
    pool_embed,
    pool_mask,
    pool_stratum,
    order,
    mask_vec,
    ratio_table,
    cot_inject,
    out_resid,
    out_hidden,
    w,
    op,
    res0,
    hin,
    saved0,
    saved,
    embed,
    cot,
    mask_in,
    stratum_in,
    order_in,
    vec_in,
    table_in,
    part,
    far,
    inner,
    near,
    summed,
    total,
    down,
    blend,
    mate_in,
    pair,
    blend_in,
    res_in,
    upd,
    hid,
    lsem,
    ssem,
    rsem,
):
    n_pipe, n_row, n_col = sizes
    p, r, c = lax.axis_index("pipe"), lax.axis_index("row"), lax.axis_index("col")
    odd = lax.rem(p, 2)
    even = odd == 0
    c_odd = lax.rem(c, 2)
    tc, tr = far.shape[1], res_in.shape[1]
    tokens = tc * n_col
    n_hid, n_feat = w.shape[1], w.shape[0]
    runs = runs_of(n_hid)
    whole = range(len(runs))
    lanes = [pl.ds(at, width) for at, width in runs]
    RES = PER_RUN * len(runs)
    MATE, SPLIT = RES + 1, RES + 3
    SPREAD = SPLIT + n_row // 2
    core, chip, n_chip = lax.rem(r, 2), r // 2, n_row // 2

    def col_at(step):
        return lax.rem(c + (step + n_col), n_col)

    def chip_at(step):
        return lax.rem(chip + step, n_chip)

    def pipe_at(step):
        return lax.rem(p + step + n_pipe, n_pipe)

    partner = p + 1 - 2 * odd
    facing = pipe_at(2 * odd - 1)
    onward = pipe_at(2 - 4 * odd)
    col_far = lax.rem(c + 2 + n_col - 4 * c_odd, n_col)

    inside = (p > 0) & (p < n_pipe - 1)
    above, below = p < n_pipe - 2, p > 1
    has_onward = (p != 1) & (p != n_pipe - 2)

    barrier = pltpu.get_barrier_semaphore()
    greeted = [{"col": col_at(s)} for s in (1, -1, 2, -2)]
    greeted += [{"pipe": partner, "col": col_at(s)} for s in (0, 2, -2)]
    greeted += [{"row": lax.rem(r + s, n_row)} for s in range(1, n_row)]
    across = [{"pipe": facing, "row": 2 * chip_at(s) + core} for s in range(n_chip)]

    def greet(devices):
        for device in devices:
            pl.semaphore_signal(barrier, inc=1, device_id=device, device_id_type=MESH)

    pl.when(inside)(lambda: greet(across))
    pl.when(above)(lambda: greet([{"pipe": pipe_at(2)}]))
    pl.when(below)(lambda: greet([{"pipe": pipe_at(-2)}]))
    greet(greeted)
    greetings = len(greeted) + jnp.where(inside, n_chip, 0)
    greetings = greetings + jnp.where(above, 1, 0) + jnp.where(below, 1, 0)

    def load(slot, src, dst):
        return pltpu.make_async_copy(src, dst, lsem.at[slot])

    row_tile = pl.ds(pl.multiple_of(r * tr, tr), tr)
    col_tile = pl.ds(pl.multiple_of(c * tc, tc), tc)
    get_w = load(0, weights.at[0], w)
    get_op = load(1, fwd_resid.at[0], op.at[0])
    get_op_odd = load(1, bwd_resid.at[0], op.at[0])
    get_res = load(2, bwd_resid.at[0, row_tile], res0)
    get_res_odd = load(2, fwd_resid.at[0, row_tile], res0)
    get_hin = load(3, bwd_hidden.at[0], hin.at[0])
    get_hin_odd = load(3, fwd_hidden.at[0], hin.at[0])
    get_saved0 = load(4, saved_pre.at[0, 0], saved0)
    get_saved = load(5, saved_pre.at[pl.ds(1, STEPS - 1), 0, col_tile], saved)

    put_op = load(13, op.at[STEPS - 1], out_resid.at[odd, 0])
    put_upd = load(14, upd, out_resid.at[1 - odd, 0])
    put_hid = load(15, hid, out_hidden.at[0])

    get_w.start()

    @pl.when(even)
    def _():
        get_op.start()
        get_hin.start()
        get_saved0.start()
        get_res.start()

    @pl.when(odd == 1)
    def _():
        get_op_odd.start()
        get_hin_odd.start()
        get_res_odd.start()

    get_saved.start()
    small = [
        load(6, pool_embed.at[:, row_tile], embed),
        load(7, cot_inject.at[:, row_tile], cot),
        load(8, pool_mask, mask_in),
        load(9, pool_stratum, stratum_in),
        load(10, order, order_in),
        load(11, mask_vec, vec_in),
        load(12, ratio_table, table_in),
    ]
    for copy in small:
        copy.start()

    started = []

    def send(k, number, src, dst, device, when=None):
        copy = pltpu.make_async_remote_copy(
            src_ref=src,
            dst_ref=dst,
            send_sem=ssem.at[k, number],
            recv_sem=rsem.at[k, number],
            device_id=device,
            device_id_type=MESH,
        )
        if when is None:
            copy.start()
        else:
            pl.when(when)(copy.start)
        started.append((copy, when))
        return copy

    def col_view(x):
        return x.reshape(n_col, tc, x.shape[-1])

    def multiply_up(k, h):
        start, width = runs[h]
        for at in range(start, start + width, 256):
            cols = pl.ds(at, min(256, start + width - at))
            out = jnp.dot(op[k], w[:, cols], preferred_element_type=F32)
            part[k, :, :, cols] = col_view(out.astype(BF16))

    def multiply_down(k, h, cols):
        out = lax.dot_general(
            hin[k, :, lanes[h]],
            w[cols, lanes[h]],
            (((1,), (1,)), ((), ())),
            preferred_element_type=F32,
        )
        if h > 0:
            out = out + down[:, cols]
        if h < len(runs) - 1:
            down[:, cols] = out
        else:
            out = out.reshape(n_chip, 2, tr, out.shape[1])
            blend[k, :, :, :, cols] = out.astype(BF16)

    def hin_tile(k, t, h):
        return hin.at[k, pl.ds(pl.multiple_of(t * tc, tc), tc), lanes[h]]

    def share(k, h, number, step, dst, to):
        src = part.at[k, col_at(step), :, lanes[h]]
        return send(k, PER_RUN * h + number, src, dst, {"col": to})

    def sum_start(k, h):
        return (
            share(k, h, FAR, 4, far.at[k, :, lanes[h]], col_far),
            share(k, h, IN_UP, 3, inner.at[k, 0, :, lanes[h]], col_at(1)),
            share(k, h, IN_DN, -3, inner.at[k, 1, :, lanes[h]], col_at(-1)),
        )

    def sum_near(k, h):
        return (
            share(k, h, NEAR_UP, 1, near.at[k, 0, :, lanes[h]], col_at(1)),
            share(k, h, NEAR_DN, -1, near.at[k, 1, :, lanes[h]], col_at(-1)),
        )

    def sum_send(k, h, number, slot, value, step):
        summed[k, slot, :, lanes[h]] = value.astype(BF16)
        src, dst = summed.at[k, slot, :, lanes[h]], total.at[k, slot, :, lanes[h]]
        device = {"col": col_at(step)}
        if k < STEPS - 1:
            device["pipe"] = partner
        return send(k, PER_RUN * h + number, src, dst, device)

    def sum_middle(k, h, arriving):
        ready(arriving)
        run = lanes[h]
        from_far = far[k, :, run].astype(F32)
        up = part[k, col_at(2), :, run].astype(F32) + inner[k, 0, :, run].astype(F32)
        up = up + jnp.where(c_odd == 0, from_far, 0.0)
        a = sum_send(k, h, SUM_UP, 0, up, 2)
        low = part[k, col_at(-2), :, run].astype(F32) + inner[k, 1, :, run].astype(F32)
        low = low + jnp.where(c_odd == 0, 0.0, from_far)
        b = sum_send(k, h, SUM_DN, 1, low, -2)
        return a, b

    def sum_own(k, h, arriving):
        ready(arriving)
        run = lanes[h]
        own = part[k, c, :, run].astype(F32) + near[k, 0, :, run].astype(F32)
        own = own + near[k, 1, :, run].astype(F32)
        if k < STEPS - 1:
            return (sum_send(k, h, SUM_OWN, 2, own, 0),)
        summed[k, 2, :, run] = own.astype(BF16)
        return ()

    def silu(v):
        return v / (1.0 + jnp.exp(-v))

    def sum_end(k, h, arriving):
        ready(arriving)
        run = lanes[h]
        own = summed if k == STEPS - 1 else total
        pre = own[k, 2, :, run].astype(F32)
        pre = pre + total[k, 0, :, run].astype(F32) + total[k, 1, :, run].astype(F32)
        from_even = even if k == STEPS - 1 else odd == 1
        return jnp.where(from_even, silu(pre), pre).astype(BF16)

    def slope(a):
        s = 1.0 / (1.0 + jnp.exp(-a))
        return s * (1.0 + a * (1.0 - s))

    def pass_on(k, h, number, tile, to):
        return send(k, PER_RUN * h + number, tile, tile, {"col": to})

    def go_far(k, h, arriving):
        value = sum_end(k, h, arriving).astype(F32)
        gate = jnp.where(even, slope(saved[k, :, lanes[h]].astype(F32)), 1.0)
        mine = hin_tile(k + 1, c, h)
        mine[...] = (value * gate).astype(BF16)
        return (
            pass_on(k, h, GO_UP2, mine, col_at(2)),
            pass_on(k, h, GO_DN2, mine, col_at(-2)),
        )

    def go_near(k, h):
        mine = hin_tile(k + 1, c, h)
        return (
            pass_on(k, h, GO_UP1, mine, col_at(1)),
            pass_on(k, h, GO_DN1, mine, col_at(-1)),
        )

    def forward(k, h, arriving):
        ready(arriving)
        below = hin_tile(k + 1, col_at(-2), h)
        above = hin_tile(k + 1, col_at(2), h)
        far_tile = hin_tile(k + 1, lax.rem(c + n_col - 2 + 4 * c_odd, n_col), h)
        return (
            pass_on(k, h, FWD_FAR, far_tile, col_far),
            pass_on(k, h, FWD_UP, below, col_at(1)),
            pass_on(k, h, FWD_DN, above, col_at(-1)),
        )

    def chip_steps(last):
        if n_chip != 4:
            return list(range(1 if last else 0, n_chip))
        return [2, 1, 3] if last else [2, 1 + 2 * odd, 0, 3 - 2 * odd]

    def mate_start(k):
        copies = []
        for n in range(2):
            cols = pl.ds(n * (n_feat // 2), n_feat // 2)
            multiply_down(k, len(runs) - 1, cols)
            src, dst = blend.at[k, :, 1 - core, :, cols], mate_in.at[k, :, :, cols]
            copies.append(send(k, MATE + n, src, dst, {"row": r + 1 - 2 * core}))
        return copies

    def blend_start(k, arriving):
        last = k == STEPS - 1
        ready(arriving)
        both = blend[k, :, core].astype(F32) + mate_in[k].astype(F32)
        pair[k] = both.astype(BF16)
        copies = []
        for i, s in enumerate(chip_steps(last)):
            to = chip_at(s)
            device = {"row": 2 * to + core}
            if not last:
                device["pipe"] = facing
            src, dst = pair.at[k, to], blend_in.at[k, i]
            copies.append(send(k, SPLIT + i, src, dst, device, None if last else inside))
        return copies

    def blend_end(k, arriving):
        last = k == STEPS - 1
        mine = (upd if last else op.at[k + 1]).at[row_tile]

        def finish():
            ready(arriving)
            new = res_in[k].astype(F32)
            if last:
                new = new + pair[k, chip].astype(F32)
            for i in range(len(chip_steps(last))):
                new = new + blend_in[k, i].astype(F32)
            mine[...] = new.astype(BF16)

        if last:
            finish()
        else:
            pl.when(inside)(finish)

            @pl.when(p == 0)
            def _():
                mine[...] = injected(k).astype(BF16)

            @pl.when(p == n_pipe - 1)
            def _():
                mine[...] = cot[k]

        copies = []
        for s in [2, 1, 3, 0] if n_chip == 4 else range(n_chip):
            for other in (0, 1) if s else (1,):
                to = 2 * chip_at(s) + core + other * (1 - 2 * core)
                copies.append(send(k, SPREAD + 2 * s + other, mine, mine, {"row": to}))
        return copies

    def pick(index, ref):
        value = ref[ref.shape[0] - 1]
        for i in range(ref.shape[0] - 1):
            value = jnp.where(index == i, ref[i], value)
        return value

    def injected(k):
        chosen = order_in[k]
        stratum = pick(chosen, stratum_in)
        mask = mask_in[pl.ds(mask_in.shape[0] - 1, 1), :]
        for i in range(mask_in.shape[0] - 1):
            mask = jnp.where(chosen == i, mask_in[pl.ds(i, 1), :], mask)
        here = lax.broadcasted_iota(jnp.int32, (tr, tokens), 0) + r * tr
        there = lax.broadcasted_iota(jnp.int32, (tr, tokens), 1)
        column = jnp.where(here == there, jnp.broadcast_to(mask, (tr, tokens)), 0)
        masked = jnp.sum(column.astype(F32), axis=1, keepdims=True) == 1.0
        table = table_in[...].astype(F32)
        strata = lax.broadcasted_iota(jnp.int32, table.shape, 0)
        condition = jnp.sum(jnp.where(strata == stratum, table, 0.0), axis=0, keepdims=True)
        vec = jnp.broadcast_to(vec_in[...].astype(F32)[None], (tr, n_feat))
        rows = jnp.where(masked, vec, pick(chosen, embed).astype(F32))
        return rows + condition

    def ready(copies):
        for copy in copies:
            copy.wait_recv()

    def starts(k):
        return [sum_start(k, h) for h in whole]

    def nears(k):
        return [sum_near(k, h) for h in whole]

    def ups(k):
        for h in whole:
            multiply_up(k, h)

    def middles(k, arriving):
        return [sum_middle(k, h, arriving[h]) for h in whole]

    def owns(k, sums, beside):
        return [sums[h] + sum_own(k, h, beside[h]) for h in whole]

    def gathers(k, arriving):
        return [go_far(k, h, arriving[h]) for h in whole]

    def goes(k):
        return [go_near(k, h) for h in whole]

    def forwards(k, arriving):
        return [forward(k, h, arriving[h]) for h in whole]

    def mates(k, arriving, beside):
        for h in whole:
            ready(arriving[h] + beside[h])
            if h < len(runs) - 1:
                for n in range(2):
                    multiply_down(k, h, pl.ds(n * (n_feat // 2), n_feat // 2))
        return mate_start(k)

    def send_res(k):
        src, dst = op.at[k, row_tile], res_in.at[k + 1]
        if k == STEPS - 2:
            return [send(k + 1, RES, src, dst, {"pipe": partner})]
        return [send(k + 1, RES, src, dst, {"pipe": onward}, has_onward)]

    nothing = [(), ()]
    get_op.wait()
    get_w.wait()
    ups(0)
    pl.semaphore_wait(barrier, greetings)
    x = starts(0)
    xn = nears(0)
    get_hin.wait()

    @pl.when(even)
    def _():
        get_saved0.wait()
        hin[0] = (hin[0].astype(F32) * slope(saved0[...].astype(F32))).astype(BF16)

    y = mates(0, nothing, nothing)
    get_res.wait()
    y_res = [send(0, RES, res0, res_in.at[0], {"pipe": facing}, inside)]
    y = blend_start(0, y)
    x_res = send_res(0)
    get_saved.wait()
    for copy in small:
        copy.wait()
    x = middles(0, x)
    x = owns(0, x, xn)
    x = gathers(0, x)
    xn = goes(0)
    y = blend_end(0, y + y_res)
    x = forwards(0, x)
    ready(y)
    ups(1)
    y = starts(1)
    yn = nears(1)
    y_res = send_res(1)
    x = mates(1, x, xn)
    x = blend_start(1, x)
    y = middles(1, y)
    y = owns(1, y, yn)
    x = blend_end(1, x + x_res)
    y = gathers(1, y)
    yn = goes(1)
    ready(x)
    ups(2)
    x = starts(2)
    y = forwards(1, y)
    xn = nears(2)
    x_res = send_res(2)
    x = middles(2, x)
    y = mates(2, y, yn)
    y = blend_start(2, y)
    x = owns(2, x, xn)
    x = gathers(2, x)
    xn = goes(2)
    x = forwards(2, x)
    y = blend_end(2, y + y_res)
    x = mates(3, x, xn)
    x = blend_start(3, x)
    ready(y)
    put_op.start()
    ups(3)
    y = starts(3)
    yn = nears(3)
    y = middles(3, y)
    y = owns(3, y, yn)
    x = blend_end(3, x + x_res)
    for h in whole:
        hid[:, lanes[h]] = sum_end(3, h, y[h])
    put_hid.start()
    ready(x)
    put_upd.start()
    for copy, when in started:
        if when is None:
            copy.wait_send()
        else:
            pl.when(when)(copy.wait_send)
    for copy in (put_op, put_upd, put_hid):
        copy.wait()


def hand_out(res, hid, out_res, out_hid, res_here, hid_here, sem):
    half = res.shape[0] // 2
    parts = [(res.at[pl.ds(i * half, half)], res_here.at[i], out_res.at[pl.ds(i * half, half)]) for i in range(2)]
    parts.append((hid, hid_here, out_hid))
    get = [pltpu.make_async_copy(a, b, sem.at[i]) for i, (a, b, _) in enumerate(parts)]
    put = [pltpu.make_async_copy(b, c, sem.at[3 + i]) for i, (_, b, c) in enumerate(parts)]
    for copy in get:
        copy.start()
    for first, second in zip(get, put):
        first.wait()
        second.start()
    for copy in put:
        copy.wait()


def solution(mesh):
    sizes = tuple(mesh.shape[a] for a in ("pipe", "row", "col"))
    n_pipe, n_row, n_col = sizes

    def shards(weights, fwd_resid, fwd_hidden, *rest):
        _, tokens, n_feat = fwd_resid.shape
        n_hid = fwd_hidden.shape[2]
        tc, tr = tokens // n_col, tokens // n_row
        pool = rest[3].shape[0]
        hbm = pl.BlockSpec(memory_space=pltpu.HBM)
        n_chip = n_row // 2
        copies = PER_RUN * len(runs_of(n_hid)) + 3 + n_chip + n_row
        out, hid_out = pl.pallas_call(
            functools.partial(relay, sizes),
            out_shape=(
                jax.ShapeDtypeStruct((2, 1, tokens, n_feat), BF16),
                jax.ShapeDtypeStruct((1, tc, n_hid), BF16),
            ),
            in_specs=[hbm] * 13,
            out_specs=(hbm, hbm),
            scratch_shapes=[
                pltpu.VMEM((n_feat, n_hid), BF16),
                pltpu.VMEM((STEPS, tokens, n_feat), BF16),
                pltpu.VMEM((tr, n_feat), BF16),
                pltpu.VMEM((STEPS, tokens, n_hid), BF16),
                pltpu.VMEM((tokens, n_hid), BF16),
                pltpu.VMEM((STEPS - 1, tc, n_hid), BF16),
                pltpu.VMEM((pool, tr, n_feat), BF16),
                pltpu.VMEM((pool, tr, n_feat), BF16),
                pltpu.VMEM((pool, tokens), jnp.int32),
                pltpu.SMEM((pool,), jnp.int32),
                pltpu.SMEM((pool,), jnp.int32),
                pltpu.VMEM((n_feat,), BF16),
                pltpu.VMEM((rest[8].shape[0], n_feat), BF16),
                pltpu.VMEM((STEPS, n_col, tc, n_hid), BF16),
                pltpu.VMEM((STEPS, tc, n_hid), BF16),
                pltpu.VMEM((STEPS, 2, tc, n_hid), BF16),
                pltpu.VMEM((STEPS, 2, tc, n_hid), BF16),
                pltpu.VMEM((STEPS, 3, tc, n_hid), BF16),
                pltpu.VMEM((STEPS, 3, tc, n_hid), BF16),
                pltpu.VMEM((tokens, n_feat), F32),
                pltpu.VMEM((STEPS, n_chip, 2, tr, n_feat), BF16),
                pltpu.VMEM((STEPS, n_chip, tr, n_feat), BF16),
                pltpu.VMEM((STEPS, n_chip, tr, n_feat), BF16),
                pltpu.VMEM((STEPS, n_chip, tr, n_feat), BF16),
                pltpu.VMEM((STEPS, tr, n_feat), BF16),
                pltpu.VMEM((tokens, n_feat), BF16),
                pltpu.VMEM((tc, n_hid), BF16),
                pltpu.SemaphoreType.DMA((16,)),
                pltpu.SemaphoreType.DMA((STEPS, copies)),
                pltpu.SemaphoreType.DMA((STEPS, copies)),
            ],
            compiler_params=pltpu.CompilerParams(
                collective_id=0, has_side_effects=True, vmem_limit_bytes=60 * 1024 * 1024
            ),
        )(weights, fwd_resid, fwd_hidden, *rest)
        return pl.pallas_call(
            hand_out,
            out_shape=(
                jax.ShapeDtypeStruct(out.shape, BF16),
                jax.ShapeDtypeStruct(hid_out.shape, BF16),
            ),
            in_specs=[hbm] * 2,
            out_specs=(hbm, hbm),
            scratch_shapes=[
                pltpu.VMEM((2, 1, 1, tokens, n_feat), BF16),
                pltpu.VMEM(hid_out.shape, BF16),
                pltpu.SemaphoreType.DMA((6,)),
            ],
            compiler_params=pltpu.CompilerParams(vmem_limit_bytes=60 * 1024 * 1024),
        )(out, hid_out)

    return jax.shard_map(
        shards,
        mesh=mesh,
        in_specs=(
            P("pipe", "col", "row"),
            P("pipe", None, "col"),
            P("pipe", None, "row"),
            P("pipe", None, "col"),
            P("pipe", None, "row"),
            P(None, "pipe", None, "row"),
            P(None, None, "col"),
            P(),
            P(),
            P(),
            P("col"),
            P(None, "col"),
            P(None, None, "col"),
        ),
        out_specs=(P(None, "pipe", None, "col"), P("pipe", "col", "row")),
        check_vma=False,
    )
```
